128 devices in a mesh: role: 4 (over y_lo, core), shard: 32 (over z, y_hi, x).
Axes of the slice: x: 4, y: 4 (y_hi: 2, y_lo: 2; y = y_hi * 2 + y_lo), z: 4, core: 2. Of those that a mesh axis runs over, the one named last changes fastest.
Arguments:
- gradient: bfloat16 [2560, 2560], P('shard', 'role'), may hold values from -1200 to 1200
- left_old: float32 [2560, 2560], P('shard', 'role'), may hold values from -1 to 10, as said below
- right_old: float32 [2560, 2560], P('shard', 'role'), may hold values from -1 to 10, as said below
- basis_old: bfloat16 [2560, 512], P('shard', 'role'), may hold values from -1 to 1
Outputs:
- left_stat: float32 [2560, 2560], P('shard', 'role')
- right_stat: float32 [2560, 2560], P('shard', 'role')
- left_basis: float32 [2560, 512], P('shard', 'role')
The draws below stay inside these ranges and needn't reach their ends.
Inputs may be any that keep to these rules, and one draw needn't show every extreme that they name: `left_old`: symmetric and positive definite. `right_old`: symmetric and positive definite.
All inputs are finite; a program needn't handle non-finite values.
Results may differ from the reference program's by a relative error of at most 0.0003.
Values may be sent and summed in bfloat16 or wider, within the bound.
A program may use at most 64 MiB of HBM per device.

```python
import jax
import jax.numpy as jnp
from jax import lax

BLK = 2560
VEC = 512


def scale_profile(key, length):
    ramp = jnp.exp(jnp.log(10.0) * jnp.arange(length, dtype=jnp.float32) / (length - 1))
    jitter = jax.random.uniform(key, (length,), jnp.float32, 0.8, 1.25)
    return ramp * jitter


def draw_gradient(key, part):
    base = jax.random.fold_in(key, 5)
    key_rows = jax.random.fold_in(base, 1)
    key_cols = jax.random.fold_in(base, 2)
    key_body = jax.random.fold_in(base, 3)
    row_scale = scale_profile(key_rows, BLK)
    col_scale = scale_profile(key_cols, BLK)
    rough = jax.random.normal(key_body, (BLK, BLK), jnp.float32)
    values = row_scale[:, None] * col_scale[None, :] * rough
    return jnp.clip(values, -1200.0, 1200.0).astype(jnp.bfloat16)


def symmetric_draw(key):
    key_diag = jax.random.fold_in(key, 1)
    key_noise = jax.random.fold_in(key, 2)
    diagonal = jnp.exp(jax.random.uniform(key_diag, (BLK,), jnp.float32, jnp.log(4.0), jnp.log(9.0)))
    noise = jax.random.normal(key_noise, (BLK, BLK), jnp.float32)
    noise = (noise + noise.T) * (1.5 / jnp.sqrt(2.0 * BLK))
    return jnp.clip(noise, -1.0, 1.0) + jnp.diag(diagonal)


def draw_left_old(key, part):
    return symmetric_draw(jax.random.fold_in(key, 21))


def draw_right_old(key, part):
    return symmetric_draw(jax.random.fold_in(key, 22))


def draw_basis_old(key, part):
    key_basis = jax.random.fold_in(key, 31)
    source = jax.random.normal(key_basis, (BLK, VEC), jnp.float32)
    orthonormal = jnp.linalg.qr(source)[0]
    return jnp.clip(orthonormal, -1.0, 1.0).astype(jnp.bfloat16)


def setup_inputs(seed: int = 0) -> dict:
    keys = jax.random.split(jax.random.key(seed), 5)
    return {
        "gradient": draw_gradient(jax.random.fold_in(keys[4], 71), 0),
        "left_old": draw_left_old(jax.random.fold_in(keys[4], 71), 0),
        "right_old": draw_right_old(jax.random.fold_in(keys[4], 71), 0),
        "basis_old": draw_basis_old(jax.random.fold_in(keys[4], 71), 0),
    }


smoothing = 0.95
clip_ratio = 4.0
epsilon_value = 1e-06

def reference(gradient, left_old, right_old, basis_old):
    gradient_wide = gradient.astype(jnp.float32)
    squares = jnp.sum(gradient_wide * gradient_wide)
    factor = jnp.minimum(1.0, clip_ratio * jnp.sqrt(jnp.float32(BLK)) / jnp.sqrt(squares + epsilon_value))
    squared = factor * factor
    left_gram = jnp.dot(gradient.astype(jnp.float32), gradient.T.astype(jnp.float32), preferred_element_type=jnp.float32)
    right_gram = jnp.dot(gradient.T.astype(jnp.float32), gradient.astype(jnp.float32), preferred_element_type=jnp.float32)
    left_stat = smoothing * left_old + (1.0 - smoothing) * squared * left_gram
    right_stat = smoothing * right_old + (1.0 - smoothing) * squared * right_gram
    power = jnp.dot(left_stat, basis_old.astype(jnp.float32), precision=lax.Precision.HIGHEST)
    gram_full = jnp.dot(power.T, power, precision=lax.Precision.HIGHEST)
    factor_lower = jnp.linalg.cholesky(gram_full)
    left_basis = jax.scipy.linalg.solve_triangular(factor_lower, power.T, lower=True).T
    return (left_stat, right_stat, left_basis)
```

```python
import functools

import jax
import jax.numpy as jnp
from jax import lax
from jax.experimental import pallas as pl
from jax.experimental.pallas import tpu as pltpu
from jax.sharding import Mesh
from jax.sharding import PartitionSpec as P

SHARD = ("shard_0", "shard_1", "shard_2")
ROLE = ("role_0", "role_1")
ROLE_SHARD = ("role_0", "role_1", "shard_0", "shard_1", "shard_2")


smoothing = 0.95
clip_ratio = 4.0
epsilon_value = 1e-06


HI = lax.Precision.HIGHEST
TN = (((0,), (0,)), ((), ()))
NT = (((1,), (1,)), ((), ()))

def dot(a, b, dims):
    return lax.dot_general(a, b, dims, precision=HI, preferred_element_type=jnp.float32)

def eliminate(d_ref):
    n = d_ref.shape[0]
    sub = lax.broadcasted_iota(jnp.int32, (8, n), 0)
    lane = lax.broadcasted_iota(jnp.int32, (8, n), 1)
    for at in range(0, n, 8):
        rows = d_ref[at:at + 8, :]
        cols = [jnp.broadcast_to(rows[:, at + j:at + j + 1], (8, n)) for j in range(8)]
        rows = jnp.where((lane >= at) & (lane < at + 8), (lane - at == sub).astype(jnp.float32), rows)
        for j in range(8):
            scale = lax.rsqrt(jnp.broadcast_to(cols[j][j:j + 1, :], (8, n)))
            below = jnp.where(sub > j, cols[j] * scale, 0.0)
            pivot = jnp.broadcast_to(rows[j:j + 1, :], (8, n)) * scale
            rows = jnp.where(sub == j, pivot, rows - below * pivot)
            for k in range(j + 1, 8):
                cols[k] = cols[k] - below * (jnp.broadcast_to(cols[k][j:j + 1, :], (8, n)) * scale)
        d_ref[at:at + 8, :] = rows
        if at + 8 < n:
            change = dot(rows, rows, TN)
            rest = d_ref[at + 8:, :]
            lanes = lax.broadcasted_iota(jnp.int32, rest.shape, 1)
            rest = jnp.where((lanes >= at) & (lanes < at + 8), 0.0, rest)
            d_ref[at + 8:, :] = rest - change[at + 8:, :]

def factor_kernel(gram_ref, w_ref, q_ref, m_ref, d_ref):
    order = gram_ref.shape[0]
    total = order + w_ref.shape[0]
    n = 128
    m_ref[:order, :] = gram_ref[...]
    m_ref[order:, :] = w_ref[...]
    row = lax.broadcasted_iota(jnp.int32, (n, n), 0)
    col = lax.broadcasted_iota(jnp.int32, (n, n), 1)
    for at in range(0, order, n):
        end = at + n
        d_ref[...] = m_ref[at:end, at:end]
        eliminate(d_ref)
        inverse = jnp.where(col <= row, d_ref[...], 0.0)
        panel = dot(m_ref[end:, at:end], inverse, NT)
        q_ref[:, at:end] = panel[order - end:, :]
        if end < order:
            m_ref[end:, end:] = m_ref[end:, end:] - dot(panel, panel[:order - end, :], NT)

def chol_q(gram, w):
    order, rows = gram.shape[0], w.shape[0]
    return pl.pallas_call(
        factor_kernel,
        out_shape=jax.ShapeDtypeStruct((rows, order), jnp.float32),
        in_specs=[pl.BlockSpec(memory_space=pltpu.VMEM)] * 2,
        out_specs=pl.BlockSpec(memory_space=pltpu.VMEM),
        scratch_shapes=[pltpu.VMEM((order + rows, order), jnp.float32), pltpu.VMEM((128, 128), jnp.float32)],
        compiler_params=pltpu.CompilerParams(vmem_limit_bytes=32 << 20),
    )(gram, w)


def over_pieces(x, axis):
    parts = lax.all_gather(x, axis)
    return parts.sum(axis=0)


def copy_for_each(x, axis):
    size = lax.axis_size(axis)
    return lax.all_to_all(jnp.broadcast_to(x[None], (size, *x.shape)), axis, 0, 0, tiled=True)


def joined_along(parts, dim):
    lengths = list(parts.shape[1:])
    lengths[dim] *= parts.shape[0]
    return jnp.moveaxis(parts, 0, dim).reshape(lengths)


def gathered_copies(x, axis, dim):
    parts = copy_for_each(x, axis)
    return joined_along(parts, dim)


def by_axis(x, axes):
    return functools.reduce(lax.psum, axes, x)


def all_blocks(x, axes, turns):
    parts = x
    for k in turns:
        parts = lax.all_gather(parts, axes[k])
    done = turns[::-1]
    back = [done.index(k) for k in range(len(axes))]
    parts = parts.transpose(*back, *range(len(axes), parts.ndim))
    return parts.reshape(-1, *x.shape)


def gathered_by_axis(x, axes, turns, dim):
    return joined_along(all_blocks(x, axes, turns), dim)


def taken_together(x, axis):
    everything = copy_for_each(x, axis)
    return jnp.sum(everything, axis=0)


def lower_gram(power_row, role_count, role_at):
    order_size = power_row.shape[1]
    tile_size = order_size // (2 * role_count)
    second_row = 2 * role_count - 1 - role_at

    def strip(tile_row):
        chosen = lax.dynamic_slice_in_dim(power_row, tile_row * tile_size, tile_size, 1)
        return lax.dot_general(
            chosen,
            power_row,
            (((0,), (0,)), ((), ())),
            precision=lax.Precision.HIGHEST,
            preferred_element_type=jnp.float32,
        )

    strip_first = strip(role_at)
    strip_second = strip(second_row)
    split_at = (role_at + 1) * tile_size
    packed_width = order_size + tile_size
    first_ext = jnp.concatenate(
        [strip_first, jnp.zeros((tile_size, tile_size), jnp.float32)], axis=1
    )
    padded_second = jnp.concatenate(
        [jnp.zeros((tile_size, order_size), jnp.float32), strip_second], axis=1
    )
    second_ext = lax.dynamic_slice_in_dim(padded_second, order_size - split_at, packed_width, 1)
    columns = lax.broadcasted_iota(jnp.int32, (tile_size, packed_width), 1)
    packed = jnp.where(columns < split_at, first_ext, second_ext)
    tile_sums = over_pieces(packed, SHARD)
    strips = gathered_copies(tile_sums, ROLE, 0)
    lower_part = jnp.zeros((order_size, order_size), jnp.float32)
    for member in range(role_count):
        packed_row = strips[member * tile_size : (member + 1) * tile_size]
        head = (member + 1) * tile_size
        other = 2 * role_count - 1 - member
        tail = (2 * role_count - member) * tile_size
        lower_part = lower_part.at[member * tile_size : head, :head].set(packed_row[:, :head])
        lower_part = lower_part.at[other * tile_size : (other + 1) * tile_size, :tail].set(
            packed_row[:, head : head + tail]
        )
    return jnp.tril(lower_part) + jnp.transpose(jnp.tril(lower_part, -1))


def on_device(gradient, left_old, right_old, basis_old):
    row_count, col_count = gradient.shape
    vec_count = basis_old.shape[1]
    order_size = row_count * lax.axis_size(SHARD)
    role_count = lax.axis_size(ROLE)
    role_at = lax.axis_index(ROLE)
    col_start = role_at * col_count
    vec_start = role_at * vec_count
    gradient_wide = gradient.astype(jnp.float32)
    squares = by_axis(jnp.sum(gradient_wide * gradient_wide), ROLE_SHARD)
    factor = jnp.minimum(
        1.0, clip_ratio * jnp.sqrt(jnp.float32(order_size)) / jnp.sqrt(squares + epsilon_value)
    )
    squared = factor * factor
    grad_row = gathered_copies(gradient, ROLE, 1)
    owned_cols = lax.all_to_all(grad_row, SHARD, split_axis=1, concat_axis=0, tiled=True)
    block_piece = gathered_by_axis(gradient, SHARD, (1, 0, 2), 0)
    left_term = lax.dot_general(
        gradient, block_piece, (((1,), (1,)), ((), ())), preferred_element_type=jnp.float32
    )
    right_acc = lax.dot_general(
        owned_cols, block_piece, (((0,), (0,)), ((), ())), preferred_element_type=jnp.float32
    )
    placed = lax.dynamic_update_slice_in_dim(
        jnp.zeros((row_count, order_size), jnp.float32), left_old, col_start, 1
    )
    left_row = taken_together((1.0 - smoothing) * squared * left_term + smoothing * placed, ROLE)
    left_stat = lax.dynamic_slice_in_dim(left_row, col_start, col_count, 1)
    right_stat = smoothing * right_old + (1.0 - smoothing) * squared * right_acc
    power_block = jnp.dot(
        left_row,
        gathered_copies(basis_old, SHARD, 0).astype(jnp.float32),
        precision=lax.Precision.HIGHEST,
    )
    power_row = gathered_copies(power_block, ROLE, 1)
    gram_full = lower_gram(power_row, role_count, role_at)
    solved = chol_q(gram_full, power_row)
    left_basis = lax.dynamic_slice_in_dim(solved, vec_start, vec_count, 1)
    return (left_stat, right_stat, left_basis)


def solution(mesh):
    finer = Mesh(
        mesh.devices.reshape(2, 2, 4, 2, 4), ("role_0", "role_1", "shard_0", "shard_1", "shard_2")
    )
    return jax.shard_map(
        on_device,
        mesh=finer,
        in_specs=(P(SHARD, ROLE), P(SHARD, ROLE), P(SHARD, ROLE), P(SHARD, ROLE)),
        out_specs=(P(SHARD, ROLE), P(SHARD, ROLE), P(SHARD, ROLE)),
        check_vma=False,
    )
```

```python
import jax
import jax.numpy as jnp
from jax import lax
from jax.experimental import pallas as pl
from jax.experimental.pallas import tpu as pltpu
from jax.sharding import Mesh
from jax.sharding import PartitionSpec as P

SHARD = ("z", "yh", "x")
ROLE = ("yl", "core")
MESH = pl.DeviceIdType.MESH

smoothing = 0.95
clip_ratio = 4.0
epsilon_value = 1e-06

HIGHEST = lax.Precision.HIGHEST
NN = (((1,), (0,)), ((), ()))
TN = (((0,), (0,)), ((), ()))
NT = (((1,), (1,)), ((), ()))


def dot(a, b, dims):
    return lax.dot_general(a, b, dims, precision=HIGHEST, preferred_element_type=jnp.float32)


def bf16_dot(a, b, dims):
    return lax.dot_general(a, b, dims, preferred_element_type=jnp.float32)


def remote(src, dst, send_sem, recv_sem, **target):
    return pltpu.make_async_remote_copy(
        src_ref=src,
        dst_ref=dst,
        send_sem=send_sem,
        recv_sem=recv_sem,
        device_id=target,
        device_id_type=MESH,
    )


def arrived(ref, sem):
    pltpu.make_async_copy(ref, ref, sem).wait()


def ring(axis, step):
    return lax.rem(lax.axis_index(axis) + (4 + step), 4)


def greet(barrier, **target):
    pl.semaphore_signal(barrier, inc=1, device_id=target, device_id_type=MESH)


def gather_kernel(pay, old, out, mine, half, recv, send, recv_mine, recv_half, send_y, local_sem):
    z, yh, x = (lax.axis_index(a) for a in SHARD)
    yl, core = (lax.axis_index(a) for a in ROLE)
    role = 2 * yl + core

    barrier = pltpu.get_barrier_semaphore()
    greeted = 0
    for dh in (0, 1):
        for dl in (0, 1):
            for dc in (0, 1):
                if dh + dl + dc:
                    greet(
                        barrier,
                        yh=lax.rem(yh + dh, 2),
                        yl=lax.rem(yl + dl, 2),
                        core=lax.rem(core + dc, 2),
                    )
                    greeted += 1
    for axis in ("z", "x"):
        for step in (1, -1):
            greet(barrier, **{axis: ring(axis, step)})
            greeted += 1
    pl.semaphore_wait(barrier, greeted)

    def unit(h, k, at_z, at_x):
        return out.at[h, k, at_z, pl.ds(pl.multiple_of(at_x * 80, 16), 80), :]

    def sem(h, k, at_z, at_x):
        return recv.at[h, k, at_z * 4 + at_x]

    waits = []

    for h in (0, 1):
        first = remote(
            pay.at[h], unit(h, yl, z, x), send_y.at[h], sem(h, yl, z, x), yh=1 - yh, yl=yh
        )
        first.start()
        waits.append(first)

        @pl.when(yl == yh)
        def _():
            pltpu.make_async_copy(pay.at[h], unit(h, yl, z, x), sem(h, yl, z, x)).start()

        @pl.when(yl != yh)
        def _():
            remote(
                pay.at[h], unit(h, yl, z, x), send_y.at[2 + h], sem(h, yl, z, x), yl=yh
            ).start()

    to_partner = remote(pay, mine.at[yl], send_y.at[4], recv_mine.at[0], yl=1 - yl)
    to_partner.start()
    waits.append(to_partner)
    own_rows = pltpu.make_async_copy(pay, mine.at[yl], local_sem.at[0])
    own_rows.start()
    own_half = pltpu.make_async_copy(old.at[yl], half.at[role], local_sem.at[1])
    own_half.start()
    to_core = remote(
        old.at[yl], half.at[role], send_y.at[5], recv_half.at[role], core=1 - core
    )
    to_core.start()
    waits.append(to_core)

    counter = [0]

    def push(h, k, at_z, at_x, axis, step):
        ref = unit(h, k, at_z, at_x)
        copy = remote(
            ref, ref, send.at[counter[0]], sem(h, k, at_z, at_x), **{axis: ring(axis, step)}
        )
        counter[0] += 1
        copy.start()
        waits.append(copy)

    def place(h, first, second):
        return (second, first) if h == 0 else (first, second)

    FIRST = ("x", "z")
    SECOND = ("z", "x")
    here = {"z": z, "x": x}

    def spread(h, k, first, second):
        at_z, at_x = place(h, first, second)
        push(h, k, at_z, at_x, SECOND[h], 1)
        push(h, k, at_z, at_x, SECOND[h], -1)

    def wait_unit(h, k, first, second):
        at_z, at_x = place(h, first, second)
        arrived(unit(h, k, at_z, at_x), sem(h, k, at_z, at_x))

    def step_one(h, k, first, second, step):
        at_z, at_x = place(h, first, second)
        push(h, k, at_z, at_x, FIRST[h], step)

    for k in (0, 1):
        for h in (0, 1):
            wait_unit(h, k, here[FIRST[h]], here[SECOND[h]])
            step_one(h, k, here[FIRST[h]], here[SECOND[h]], 1)
            step_one(h, k, here[FIRST[h]], here[SECOND[h]], -1)
    for k in (0, 1):
        for h in (0, 1):
            spread(h, k, here[FIRST[h]], here[SECOND[h]])
    for k in (0, 1):
        onward = 1 if k == 0 else -1
        for h in (0, 1):
            behind = ring(FIRST[h], -onward)
            wait_unit(h, k, behind, here[SECOND[h]])
            step_one(h, k, behind, here[SECOND[h]], onward)
    for k in (0, 1):
        onward = 1 if k == 0 else -1
        for h in (0, 1):
            spread(h, k, ring(FIRST[h], -onward), here[SECOND[h]])
    for k in (0, 1):
        onward = 1 if k == 0 else -1
        for h in (0, 1):
            ahead = ring(FIRST[h], onward)
            wait_unit(h, k, ahead, here[SECOND[h]])
            spread(h, k, ahead, here[SECOND[h]])
    for k in (0, 1):
        for h in (0, 1):
            far = ring(FIRST[h], 2)
            wait_unit(h, k, far, here[SECOND[h]])
            spread(h, k, far, here[SECOND[h]])

    for dc in (0, 1):
        across = remote(
            old.at[1 - yl],
            half.at[role],
            send_y.at[6 + dc],
            recv_half.at[role],
            yl=1 - yl,
            core=lax.rem(core + dc, 2),
        )
        across.start()
        waits.append(across)

    def column(h, k, turn):
        onward = 1 if k == 0 else -1
        return ring(FIRST[h], (0, -onward, onward, 2)[turn])

    for turn in range(4):
        for k in (0, 1):
            onward = 1 if k == 0 else -1
            for h in (0, 1):
                behind = ring(SECOND[h], -onward)
                first = column(h, k, turn)
                wait_unit(h, k, first, behind)
                at_z, at_x = place(h, first, behind)
                push(h, k, at_z, at_x, SECOND[h], onward)
    for turn in range(4):
        for k in (0, 1):
            onward = 1 if k == 0 else -1
            for h in (0, 1):
                first = column(h, k, turn)
                wait_unit(h, k, first, ring(SECOND[h], onward))
                wait_unit(h, k, first, ring(SECOND[h], 2))

    own_rows.wait()
    own_half.wait()
    arrived(mine.at[1 - yl], recv_mine.at[0])
    for dl in (0, 1):
        for dc in (0, 1):
            if dl + dc:
                other = 2 * lax.rem(yl + dl, 2) + lax.rem(core + dc, 2)
                arrived(half.at[other], recv_half.at[other])
    for copy in waits:
        copy.wait_send()

    @pl.when(yl != yh)
    def _():
        for h in (0, 1):
            remote(
                pay.at[h], unit(h, yl, z, x), send_y.at[2 + h], sem(h, yl, z, x), yl=yh
            ).wait_send()


def gather(pay, old):
    return pl.pallas_call(
        gather_kernel,
        out_shape=(
            jax.ShapeDtypeStruct((2, 2, 4, 320, 384), jnp.bfloat16),
            jax.ShapeDtypeStruct((2, 2, 80, 384), jnp.bfloat16),
            jax.ShapeDtypeStruct((4, 80, 320), jnp.float32),
        ),
        in_specs=[pl.BlockSpec(memory_space=pl.ANY)] * 2,
        out_specs=(pl.BlockSpec(memory_space=pl.ANY),) * 3,
        scratch_shapes=[
            pltpu.SemaphoreType.DMA((2, 2, 16)),
            pltpu.SemaphoreType.DMA((64,)),
            pltpu.SemaphoreType.DMA((1,)),
            pltpu.SemaphoreType.DMA((4,)),
            pltpu.SemaphoreType.DMA((8,)),
            pltpu.SemaphoreType.DMA((2,)),
        ],
        compiler_params=pltpu.CompilerParams(collective_id=0, has_side_effects=True),
    )(pay, old)


def parts_of(x):
    high = x.astype(jnp.bfloat16)
    rest = x - high.astype(jnp.float32)
    middle = rest.astype(jnp.bfloat16)
    low = (rest - middle.astype(jnp.float32)).astype(jnp.bfloat16)
    return high, middle, low


def power_kernel(
    blocks, mine, half,
    gram, power, left, squares,
    partial, partial_in, stat, power_part, power_in, chunk, pieces,
    send_core, recv_core, send_sq, recv_sq, send_y, recv_y, send_w, recv_w, send_left, recv_left,
    send_rs, recv_rs, send_ag, recv_ag, send_g, recv_g,
):
    z, yh, x = (lax.axis_index(a) for a in SHARD)
    yl, core = (lax.axis_index(a) for a in ROLE)
    role = 2 * yl + core
    across = 2 * (1 - yl) + core
    shard = z * 8 + yh * 4 + x

    def peer(step):
        other = lax.rem(shard + step, 32)
        return other, {"z": other // 8, "yh": lax.rem(other // 4, 2), "x": lax.rem(other, 4)}

    barrier = pltpu.get_barrier_semaphore()

    def greet_step(step, _):
        other, place = peer(step)
        greet(barrier, **place)
        greet(barrier, yl=1 - yl, **place)
        return 0

    lax.fori_loop(1, 32, greet_step, 0)
    greet(barrier, yl=1 - yl)
    greet(barrier, core=1 - core)
    greet(barrier, yl=1 - yl, core=1 - core)

    def squares_of(i, total):
        k, at_z = i // 4, lax.rem(i, 4)

        def rows_step(j, total):
            rows = pl.ds(pl.multiple_of(j * 16, 16), 16)
            a = blocks[0, k, at_z, rows, :].astype(jnp.float32)
            b = blocks[1, k, at_z, rows, :256].astype(jnp.float32)
            a = a * a
            b = b * b
            wide = a[:, :128] + a[:, 128:256] + a[:, 256:] + b[:, :128] + b[:, 128:]
            return total + wide[:8] + wide[8:]

        return lax.fori_loop(0, 20, rows_step, total, unroll=4)

    squares[role] = lax.fori_loop(0, 8, squares_of, jnp.zeros((8, 128), jnp.float32))

    pl.semaphore_wait(barrier, 65)

    sq_copies = []
    for n, (dl, dc) in enumerate(((1, 0), (0, 1), (1, 1))):
        copy = remote(
            squares.at[role],
            squares.at[role],
            send_sq.at[n],
            recv_sq.at[role],
            yl=lax.rem(yl + dl, 2),
            core=lax.rem(core + dc, 2),
        )
        copy.start()
        sq_copies.append(copy)

    core_copies = []
    for at_z in range(4):
        total = jnp.zeros((80, 320), jnp.float32)
        for k in (0, 1):
            total += bf16_dot(mine[k, 0], blocks[0, k, at_z], NT)
            total += bf16_dot(mine[k, 1, :, :256], blocks[1, k, at_z, :, :256], NT)
        partial[at_z] = total
        copy = remote(
            partial.at[at_z],
            partial_in.at[at_z],
            send_core.at[at_z],
            recv_core.at[at_z],
            core=1 - core,
        )
        copy.start()
        core_copies.append(copy)

    for dl, dc in ((1, 0), (0, 1), (1, 1)):
        other = 2 * lax.rem(yl + dl, 2) + lax.rem(core + dc, 2)
        arrived(squares.at[other], recv_sq.at[other])
    all_squares = jnp.sum(squares[0] + squares[1] + squares[2] + squares[3])
    order_size = jnp.float32(2560)
    factor = jnp.minimum(
        1.0,
        clip_ratio
        * jnp.sqrt(order_size)
        / jnp.sqrt(jnp.full((8, 128), all_squares + epsilon_value, jnp.float32)),
    )
    weight = ((1.0 - smoothing) * (factor * factor))[:1, :1]

    sums = [jnp.zeros((80, 128), jnp.float32)] * 2
    for at_z in range(4):
        core_copies[at_z].wait_recv()
        value = smoothing * half[at_z] + weight * (partial[at_z] + partial_in[at_z])
        stat[at_z] = value
        stacked = jnp.concatenate(parts_of(value), axis=0)
        for k in (0, 1):
            product = bf16_dot(stacked, blocks[1, k, at_z, :, 256:], NN)
            sums[k] = sums[k] + (product[:80] + product[80:160] + product[160:])
    for k in (0, 1):
        power_part[k] = sums[k]
    y_copy = remote(power_part, power_in, send_y.at[0], recv_y.at[0], yl=1 - yl)
    y_copy.start()
    left[yl] = stat[role]
    left_copy = remote(stat.at[across], left.at[yl], send_left.at[0], recv_left.at[0], yl=1 - yl)
    left_copy.start()

    y_copy.wait_recv()
    w_copies = []
    for k in (0, 1):
        slot = 2 * k + core
        power[slot] = power_part[k] + power_in[k]
        copy = remote(power.at[slot], power.at[slot], send_w.at[k], recv_w.at[slot], core=1 - core)
        copy.start()
        w_copies.append(copy)
    for k in (0, 1):
        slot = 2 * k + 1 - core
        arrived(power.at[slot], recv_w.at[slot])

    columns = power[role]
    for pair in (0, 1):
        strip = dot(columns, jnp.concatenate([power[2 * pair], power[2 * pair + 1]], axis=1), TN)
        for t in range(16):
            chunk[2 * t + pair] = strip[8 * t : 8 * t + 8, :]

    def scatter_copy(step):
        other, place = peer(step)
        return remote(
            chunk.at[other], pieces.at[shard], send_rs.at[other], recv_rs.at[shard], **place
        )

    def scatter_start(step, _):
        scatter_copy(step).start()
        return 0

    lax.fori_loop(1, 32, scatter_start, 0)

    def scatter_arrive(step, total):
        other, _ = peer(step)
        arrived(pieces.at[other], recv_rs.at[other])
        return total + pieces[other]

    gram[role, shard] = lax.fori_loop(1, 32, scatter_arrive, chunk[shard])

    def spread_copy(step, flip):
        other, place = peer(step)
        if flip:
            place = dict(place, yl=1 - yl)
        return remote(
            gram.at[role, shard],
            gram.at[role, shard],
            send_ag.at[flip, other],
            recv_ag.at[flip, shard],
            **place,
        )

    def spread_start(step, _):
        spread_copy(step, 1).start()
        spread_copy(step, 0).start()
        return 0

    spread_copy(0, 1).start()
    lax.fori_loop(1, 32, spread_start, 0)

    arrived(gram.at[across, shard], recv_ag.at[1, shard])

    def spread_arrive(step, _):
        other, _ = peer(step)
        arrived(gram.at[across, other], recv_ag.at[1, other])
        arrived(gram.at[role, other], recv_ag.at[0, other])
        return 0

    lax.fori_loop(1, 32, spread_arrive, 0)

    g_copies = []
    for k in (0, 1):
        slot = 2 * k + core
        copy = remote(gram.at[slot], gram.at[slot], send_g.at[k], recv_g.at[slot], core=1 - core)
        copy.start()
        g_copies.append(copy)
    for k in (0, 1):
        slot = 2 * k + 1 - core
        arrived(gram.at[slot], recv_g.at[slot])

    arrived(left.at[1 - yl], recv_left.at[0])

    def drain(step, _):
        scatter_copy(step).wait_send()
        spread_copy(step, 1).wait_send()
        spread_copy(step, 0).wait_send()
        return 0

    lax.fori_loop(1, 32, drain, 0)
    spread_copy(0, 1).wait_send()
    for copy in sq_copies + core_copies + [y_copy, left_copy] + w_copies + g_copies:
        copy.wait_send()


def power_and_gram(blocks, mine, half):
    vmem = pl.BlockSpec(memory_space=pltpu.VMEM)
    dma = pltpu.SemaphoreType.DMA
    f32 = jnp.float32
    return pl.pallas_call(
        power_kernel,
        out_shape=(
            jax.ShapeDtypeStruct((4, 32, 8, 256), f32),
            jax.ShapeDtypeStruct((4, 80, 128), f32),
            jax.ShapeDtypeStruct((2, 80, 320), f32),
            jax.ShapeDtypeStruct((4, 8, 128), f32),
        ),
        in_specs=[vmem] * 3,
        out_specs=(vmem,) * 4,
        scratch_shapes=[
            pltpu.VMEM((4, 80, 320), f32),
            pltpu.VMEM((4, 80, 320), f32),
            pltpu.VMEM((4, 80, 320), f32),
            pltpu.VMEM((2, 80, 128), f32),
            pltpu.VMEM((2, 80, 128), f32),
            pltpu.VMEM((32, 8, 256), f32),
            pltpu.VMEM((32, 8, 256), f32),
            dma((4,)), dma((4,)),
            dma((3,)), dma((4,)),
            dma((1,)), dma((1,)),
            dma((2,)), dma((4,)),
            dma((1,)), dma((1,)),
            dma((32,)), dma((32,)),
            dma((2, 32)), dma((2, 32)),
            dma((2,)), dma((4,)),
        ],
        compiler_params=pltpu.CompilerParams(
            collective_id=1, has_side_effects=True, vmem_limit_bytes=40 << 20
        ),
    )(blocks, mine, half)


def eliminate(d_ref):
    n = d_ref.shape[0]
    sub = lax.broadcasted_iota(jnp.int32, (8, n), 0)
    lane = lax.broadcasted_iota(jnp.int32, (8, n), 1)
    for at in range(0, n, 8):
        rows = d_ref[at : at + 8, :]
        cols = [jnp.broadcast_to(rows[:, at + j : at + j + 1], (8, n)) for j in range(8)]
        inside = (lane >= at) & (lane < at + 8)
        rows = jnp.where(inside, (lane - at == sub).astype(jnp.float32), rows)
        for j in range(8):
            scale = lax.rsqrt(jnp.broadcast_to(cols[j][j : j + 1, :], (8, n)))
            below = jnp.where(sub > j, cols[j] * scale, 0.0)
            pivot = jnp.broadcast_to(rows[j : j + 1, :], (8, n)) * scale
            rows = jnp.where(sub == j, pivot, rows - below * pivot)
            for k in range(j + 1, 8):
                row = jnp.broadcast_to(cols[k][j : j + 1, :], (8, n))
                cols[k] = cols[k] - below * (row * scale)
        d_ref[at : at + 8, :] = rows
        if at + 8 < n:
            change = dot(rows, rows, TN)
            rest = d_ref[at + 8 :, :]
            lanes = lax.broadcasted_iota(jnp.int32, rest.shape, 1)
            rest = jnp.where((lanes >= at) & (lanes < at + 8), 0.0, rest)
            d_ref[at + 8 :, :] = rest - change[at + 8 :, :]


def factor_kernel(gram_ref, w_ref, q_ref, m_ref, d_ref):
    order = 512
    n = 128
    role = 2 * lax.axis_index("yl") + lax.axis_index("core")
    for r in range(4):
        for t in range(16):
            for pair in (0, 1):
                at = n * r + 8 * t
                m_ref[at : at + 8, 256 * pair : 256 * pair + 256] = gram_ref[r, 2 * t + pair]
        m_ref[order:, n * r : n * r + n] = w_ref[r]
    row = lax.broadcasted_iota(jnp.int32, (n, n), 0)
    col = lax.broadcasted_iota(jnp.int32, (n, n), 1)
    for at in range(0, order, n):
        end = at + n
        d_ref[...] = m_ref[at:end, at:end]
        eliminate(d_ref)
        inverse = jnp.where(col <= row, d_ref[...], 0.0)
        panel = dot(m_ref[end:, at:end], inverse, NT)

        @pl.when(role == at // n)
        def _():
            q_ref[...] = panel[order - end :, :]

        if end < order:
            m_ref[end:, end:] = m_ref[end:, end:] - dot(panel, panel[: order - end, :], NT)


def factor(gram, power):
    return pl.pallas_call(
        factor_kernel,
        out_shape=jax.ShapeDtypeStruct((80, 128), jnp.float32),
        in_specs=[pl.BlockSpec(memory_space=pltpu.VMEM)] * 2,
        out_specs=pl.BlockSpec(memory_space=pltpu.VMEM),
        scratch_shapes=[pltpu.VMEM((592, 512), jnp.float32), pltpu.VMEM((128, 128), jnp.float32)],
        compiler_params=pltpu.CompilerParams(vmem_limit_bytes=32 << 20),
        cost_estimate=pl.CostEstimate(
            flops=20_000_000_000, bytes_accessed=1_500_000, transcendentals=0
        ),
    )(gram, power)


def on_device(gradient, left_old, right_old, basis_old):
    z, yh, x = (lax.axis_index(a) for a in SHARD)
    yl, core = (lax.axis_index(a) for a in ROLE)
    pay = jnp.stack(
        [gradient[:, :384], jnp.concatenate([gradient[:, 384:], basis_old], axis=1)]
    )
    old = jnp.stack([left_old[:, :320], left_old[:, 320:]])
    blocks, mine, half = gather(pay, old)
    gram, power, left, squares = power_and_gram(blocks, mine, half)
    left_basis = factor(gram, power)
    left_stat = jnp.concatenate([left[0], left[1]], axis=1)

    columns = jnp.concatenate(
        [blocks[0].reshape(2, 1280, 384), blocks[1].reshape(2, 1280, 384)[:, :, :256]], axis=2
    )
    kept = lax.dynamic_index_in_dim(columns, z // 2, 0, keepdims=False)
    kept = lax.dynamic_slice_in_dim(kept, 80 * (4 * yh + x), 80, 1)
    swapped = lax.ppermute(kept, "core", [(0, 1), (1, 0)])
    kept = jnp.where(core == lax.rem(z, 2), kept, swapped)
    right = lax.dot_general(
        kept, columns, (((0,), (1,)), ((), ())), preferred_element_type=jnp.float32
    )
    theirs = lax.dynamic_index_in_dim(right, 1 - yl, 1, keepdims=False)
    ours = lax.dynamic_index_in_dim(right, yl, 1, keepdims=False)
    right_gram = ours + lax.ppermute(theirs, "yl", [(0, 1), (1, 0)])
    total = jnp.sum(squares)
    factor_now = jnp.minimum(
        1.0, clip_ratio * jnp.sqrt(jnp.float32(2560)) / jnp.sqrt(total + epsilon_value)
    )
    right_stat = smoothing * right_old + (1.0 - smoothing) * (factor_now * factor_now) * right_gram
    return (left_stat, right_stat, left_basis)


def solution(mesh):
    finer = Mesh(mesh.devices.reshape(2, 2, 4, 2, 4), ("yl", "core", "z", "yh", "x"))
    return jax.shard_map(
        on_device,
        mesh=finer,
        in_specs=(P(SHARD, ROLE),) * 4,
        out_specs=(P(SHARD, ROLE),) * 3,
        check_vma=False,
    )
```

```python
import jax
import jax.numpy as jnp
from jax import lax
from jax.experimental import pallas as pl
from jax.experimental.pallas import tpu as pltpu
from jax.sharding import Mesh
from jax.sharding import PartitionSpec as P

SHARD = ("z", "yh", "x")
ROLE = ("yl", "core")
MESH = pl.DeviceIdType.MESH

smoothing = 0.95
clip_ratio = 4.0
epsilon_value = 1e-06

NN = (((1,), (0,)), ((), ()))
TN = (((0,), (0,)), ((), ()))
NT = (((1,), (1,)), ((), ()))


def bf16_dot(a, b, dims):
    return lax.dot_general(a, b, dims, preferred_element_type=jnp.float32)


def remote(src, dst, send_sem, recv_sem, **target):
    return pltpu.make_async_remote_copy(
        src_ref=src,
        dst_ref=dst,
        send_sem=send_sem,
        recv_sem=recv_sem,
        device_id=target,
        device_id_type=MESH,
    )


def arrived(ref, sem):
    pltpu.make_async_copy(ref, ref, sem).wait()


def ring(axis, step):
    return lax.rem(lax.axis_index(axis) + (4 + step), 4)


def greet(barrier, **target):
    pl.semaphore_signal(barrier, inc=1, device_id=target, device_id_type=MESH)


def stat_weight(squares):
    full = jnp.full((8, 128), squares + epsilon_value, jnp.float32)
    factor = jnp.minimum(1.0, clip_ratio * jnp.sqrt(jnp.float32(2560)) / jnp.sqrt(full))
    return (1.0 - smoothing) * (factor * factor)


def parts_of(x):
    high = x.astype(jnp.bfloat16)
    rest = x - high.astype(jnp.float32)
    middle = rest.astype(jnp.bfloat16)
    low = (rest - middle.astype(jnp.float32)).astype(jnp.bfloat16)
    return high, middle, low


def full_dot(a, b, dims):
    a_axis, b_axis = dims[0][0][0], dims[0][1][0]
    ah, am, al = parts_of(a)
    bh, bm, bl = (ah, am, al) if b is a else parts_of(b)
    left = jnp.concatenate([ah, ah, am, ah, al, am], axis=a_axis)
    right = jnp.concatenate([bh, bm, bh, bl, bh, bm], axis=b_axis)
    return bf16_dot(left, right, dims)


def main_kernel(
    gradient, basis, left_old,
    gram, power, left, squares, ours, theirs,
    blocks, mine, half, sq_sum, kept, right_out, partial, partial_in, stat, power_part, power_in, chunk, pieces,
    give, recv, send, send_y, recv_mine, recv_half, local_sem,
    send_core, recv_core, send_sq, recv_sq, send_w, recv_w, send_one, recv_one,
    send_rs, recv_rs, send_ag, recv_ag, send_g, recv_g,
):
    z, yh, x = (lax.axis_index(a) for a in SHARD)
    yl, core = (lax.axis_index(a) for a in ROLE)
    role = 2 * yl + core
    across = 2 * (1 - yl) + core
    shard = z * 8 + yh * 4 + x

    def peer(step):
        other = lax.rem(shard + step, 32)
        return other, {"z": other // 8, "yh": lax.rem(other // 4, 2), "x": lax.rem(other, 4)}

    barrier = pltpu.get_barrier_semaphore()

    def greet_step(step, _):
        other, place = peer(step)
        greet(barrier, **place)
        greet(barrier, yl=1 - yl, **place)
        return 0

    greet(barrier, yl=1 - yl)
    greet(barrier, core=1 - core)
    greet(barrier, yl=1 - yl, core=1 - core)
    lax.fori_loop(1, 32, greet_step, 0)

    own_rows = pltpu.make_async_copy(gradient, mine.at[yl], local_sem.at[0])
    own_rows.start()
    own_half = pltpu.make_async_copy(
        left_old.at[:, pl.ds(pl.multiple_of(256 * yl, 128), 384)], half.at[role], local_sem.at[1]
    )
    own_half.start()
    sq_sum[...] = jnp.zeros((8, 128), jnp.float32)
    waits = []

    pl.semaphore_wait(barrier, 65)

    def unit(h, k, at_z, at_x):
        return blocks.at[h, k, at_z, pl.ds(pl.multiple_of(at_x * 80, 16), 80), :]

    def sem(h, k, at_z, at_x):
        return recv.at[h, k, at_z * 4 + at_x]

    def pieces_of(h):
        to = unit(h, yl, z, x)
        if h == 0:
            return [(gradient.at[:, :384], to)]
        return [(gradient.at[:, 384:], to.at[:, :256]), (basis, to.at[:, 256:])]

    def give_copy(h, n, src, dst):
        return remote(src, dst, give.at[0, h + n], sem(h, yl, z, x), yh=1 - yh, yl=yh)

    def lend_copy(h, n, src, dst):
        return remote(src, dst, give.at[1, h + n], sem(h, yl, z, x), yl=yh)

    for h in (0, 1):
        for n, (src, dst) in enumerate(pieces_of(h)):
            copy = give_copy(h, n, src, dst)
            copy.start()
            waits.append(copy)

            @pl.when(yl == yh)
            def _():
                pltpu.make_async_copy(src, dst, sem(h, yl, z, x)).start()

            @pl.when(yl != yh)
            def _():
                lend_copy(h, n, src, dst).start()

    to_partner = remote(gradient, mine.at[yl], send_y.at[0], recv_mine.at[0], yl=1 - yl)
    to_partner.start()
    waits.append(to_partner)
    to_core = remote(
        left_old.at[:, pl.ds(pl.multiple_of(256 * yl, 128), 384)],
        half.at[role],
        send_y.at[1],
        recv_half.at[role],
        core=1 - core,
    )
    to_core.start()
    waits.append(to_core)

    counter = [0]

    def push(h, k, at_z, at_x, axis, step):
        ref = unit(h, k, at_z, at_x)
        copy = remote(
            ref, ref, send.at[counter[0]], sem(h, k, at_z, at_x), **{axis: ring(axis, step)}
        )
        counter[0] += 1
        copy.start()
        waits.append(copy)

    def place(h, first, second):
        return (second, first) if h == 0 else (first, second)

    FIRST = ("x", "z")
    SECOND = ("z", "x")
    here = {"z": z, "x": x}

    def spread(h, k, first, second):
        at_z, at_x = place(h, first, second)
        push(h, k, at_z, at_x, SECOND[h], 1)
        push(h, k, at_z, at_x, SECOND[h], -1)

    def wait_unit(h, k, first, second):
        at_z, at_x = place(h, first, second)
        arrived(unit(h, k, at_z, at_x), sem(h, k, at_z, at_x))

    def add_squares(h, k, first, second):
        at_z, at_x = place(h, first, second)
        width = 384 if h == 0 else 256
        start = pl.multiple_of(at_x * 80, 16)
        value = blocks[h, k, at_z, pl.ds(start, 80), :width].astype(jnp.float32)
        value = value * value
        wide = value[:, :128]
        for lane in range(128, width, 128):
            wide = wide + value[:, lane : lane + 128]
        total = wide[:8]
        for row in range(8, 80, 8):
            total = total + wide[row : row + 8]
        sq_sum[...] += total

    def step_one(h, k, first, second, step):
        at_z, at_x = place(h, first, second)
        push(h, k, at_z, at_x, FIRST[h], step)

    both = [(k, h, 1 if k == 0 else -1) for k in (0, 1) for h in (0, 1)]

    for k, h, onward in both:
        wait_unit(h, k, here[FIRST[h]], here[SECOND[h]])
        step_one(h, k, here[FIRST[h]], here[SECOND[h]], 1)
        step_one(h, k, here[FIRST[h]], here[SECOND[h]], -1)
    for k, h, onward in both:
        spread(h, k, here[FIRST[h]], here[SECOND[h]])
    for k, h, onward in both:
        add_squares(h, k, here[FIRST[h]], here[SECOND[h]])
    for k, h, onward in both:
        behind = ring(FIRST[h], -onward)
        wait_unit(h, k, behind, here[SECOND[h]])
        step_one(h, k, behind, here[SECOND[h]], onward)
    for k, h, onward in both:
        spread(h, k, ring(FIRST[h], -onward), here[SECOND[h]])
    for k, h, onward in both:
        ahead = ring(FIRST[h], onward)
        wait_unit(h, k, ahead, here[SECOND[h]])
        spread(h, k, ahead, here[SECOND[h]])
    for k, h, onward in both:
        add_squares(h, k, ring(FIRST[h], -onward), here[SECOND[h]])
        add_squares(h, k, ring(FIRST[h], onward), here[SECOND[h]])
    for k, h, onward in both:
        far = ring(FIRST[h], 2)
        wait_unit(h, k, far, here[SECOND[h]])
        spread(h, k, far, here[SECOND[h]])

    for dc in (0, 1):
        over = remote(
            left_old.at[:, pl.ds(pl.multiple_of(256 * (1 - yl), 128), 384)],
            half.at[role],
            send_y.at[2 + dc],
            recv_half.at[role],
            yl=1 - yl,
            core=lax.rem(core + dc, 2),
        )
        over.start()
        waits.append(over)
    for k, h, onward in both:
        add_squares(h, k, ring(FIRST[h], 2), here[SECOND[h]])

    def column(h, k, turn):
        onward = 1 if k == 0 else -1
        return ring(FIRST[h], (0, -onward, onward, 2)[turn])

    for turn in range(4):
        for k, h, onward in both:
            behind = ring(SECOND[h], -onward)
            first = column(h, k, turn)
            wait_unit(h, k, first, behind)
            at_z, at_x = place(h, first, behind)
            push(h, k, at_z, at_x, SECOND[h], onward)
        for k, h, onward in both:
            add_squares(h, k, column(h, k, turn), ring(SECOND[h], -onward))
    for turn in range(4):
        for k, h, onward in both:
            first = column(h, k, turn)
            ahead, far = ring(SECOND[h], onward), ring(SECOND[h], 2)
            wait_unit(h, k, first, ahead)
            add_squares(h, k, first, ahead)
            wait_unit(h, k, first, far)
            add_squares(h, k, first, far)
    own_rows.wait()
    arrived(mine.at[1 - yl], recv_mine.at[0])

    squares[role] = sq_sum[...]
    sq_copies = []
    for n, (dl, dc) in enumerate(((1, 0), (0, 1), (1, 1))):
        copy = remote(
            squares.at[role],
            squares.at[role],
            send_sq.at[n],
            recv_sq.at[role],
            yl=lax.rem(yl + dl, 2),
            core=lax.rem(core + dc, 2),
        )
        copy.start()
        sq_copies.append(copy)
    core_copies = []
    for at_z in range(4):
        total = jnp.zeros((80, 320), jnp.float32)
        for k in (0, 1):
            total += bf16_dot(mine[k, :, :384], blocks[0, k, at_z], NT)
            total += bf16_dot(mine[k, :, 384:], blocks[1, k, at_z, :, :256], NT)
        partial[at_z] = total
        copy = remote(
            partial.at[at_z],
            partial_in.at[at_z],
            send_core.at[at_z],
            recv_core.at[at_z],
            core=1 - core,
        )
        copy.start()
        core_copies.append(copy)

    own_half.wait()
    for dl, dc in ((0, 1), (1, 0), (1, 1)):
        other = 2 * lax.rem(yl + dl, 2) + lax.rem(core + dc, 2)
        arrived(half.at[other], recv_half.at[other])
        arrived(squares.at[other], recv_sq.at[other])
    all_squares = jnp.sum(squares[0] + squares[1] + squares[2] + squares[3])
    weight = stat_weight(all_squares)[:1, :1]

    sums = [jnp.zeros((80, 128), jnp.float32)] * 2
    for at_z in range(4):
        core_copies[at_z].wait_recv()
        held = half[at_z]
        held = jnp.where(yl == 0, held[:, :320], held[:, 64:])
        value = smoothing * held + weight * (partial[at_z] + partial_in[at_z])
        stat[at_z] = value
        stacked = jnp.concatenate(parts_of(value), axis=0)
        for k in (0, 1):
            product = bf16_dot(stacked, blocks[1, k, at_z, :, 256:], NN)
            sums[k] = sums[k] + (product[:80] + product[80:160] + product[160:])
    for k in (0, 1):
        power_part[k] = sums[k]
    y_copy = remote(power_part, power_in, send_one.at[0], recv_one.at[0], yl=1 - yl)
    y_copy.start()
    left[yl] = stat[role]
    left_copy = remote(stat.at[across], left.at[yl], send_one.at[1], recv_one.at[1], yl=1 - yl)
    left_copy.start()

    has_columns = core == lax.rem(z, 2)
    kept_copy = remote(kept, kept, send_one.at[2], recv_one.at[2], core=1 - core)

    @pl.when(has_columns)
    def _():
        offset = 80 * (4 * yh + x)
        row = lax.broadcasted_iota(jnp.int32, (80, 640), 0)
        col = lax.broadcasted_iota(jnp.int32, (80, 640), 1)
        pick = jnp.where(col == row + offset, 1.0, 0.0).astype(jnp.bfloat16)
        for at_z in range(4):
            chosen = bf16_dot(pick[:, :384], blocks[0, z // 2, at_z], NT)
            chosen += bf16_dot(pick[:, 384:], blocks[1, z // 2, at_z, :, :256], NT)
            kept[at_z] = chosen.astype(jnp.bfloat16)
        kept_copy.start()

    y_copy.wait_recv()
    w_copies = []
    for k in (0, 1):
        slot = 2 * k + core
        power[slot] = power_part[k] + power_in[k]
        copy = remote(power.at[slot], power.at[slot], send_w.at[k], recv_w.at[slot], core=1 - core)
        copy.start()
        w_copies.append(copy)
    for k in (0, 1):
        slot = 2 * k + 1 - core
        arrived(power.at[slot], recv_w.at[slot])

    columns = power[role]
    for pair in (0, 1):
        strip = full_dot(columns, jnp.concatenate([power[2 * pair], power[2 * pair + 1]], axis=1), TN)
        for t in range(16):
            chunk[2 * t + pair] = strip[8 * t : 8 * t + 8, :]

    def scatter_copy(step):
        other, place = peer(step)
        return remote(
            chunk.at[other], pieces.at[shard], send_rs.at[other], recv_rs.at[shard], **place
        )

    def scatter_start(step, _):
        scatter_copy(step).start()
        return 0

    lax.fori_loop(1, 32, scatter_start, 0)

    @pl.when(jnp.logical_not(has_columns))
    def _():
        arrived(kept, recv_one.at[2])

    def right_product(k, out):
        for h, width in ((0, 384), (1, 256)):
            total = jnp.zeros((80, width), jnp.float32)
            for at_z in range(4):
                total += bf16_dot(kept[at_z], blocks[h, k, at_z, :, :width], NN)
            out[:, 384 * h : 384 * h + width] = total

    right_product(1 - yl, right_out)
    right_copy = remote(right_out, theirs, send_one.at[3], recv_one.at[3], yl=1 - yl)
    right_copy.start()

    def scatter_arrive(step, total):
        other, _ = peer(step)
        arrived(pieces.at[other], recv_rs.at[other])
        return total + pieces[other]

    gram[role, shard] = lax.fori_loop(1, 32, scatter_arrive, chunk[shard])

    def spread_copy(step, flip):
        other, place = peer(step)
        if flip:
            place = dict(place, yl=1 - yl)
        return remote(
            gram.at[role, shard],
            gram.at[role, shard],
            send_ag.at[flip, other],
            recv_ag.at[flip, shard],
            **place,
        )

    def spread_start(step, _):
        spread_copy(step, 1).start()
        spread_copy(step, 0).start()
        return 0

    spread_copy(0, 1).start()
    lax.fori_loop(1, 32, spread_start, 0)
    right_product(yl, ours)

    arrived(gram.at[across, shard], recv_ag.at[1, shard])

    def spread_arrive(step, _):
        other, _ = peer(step)
        arrived(gram.at[across, other], recv_ag.at[1, other])
        arrived(gram.at[role, other], recv_ag.at[0, other])
        return 0

    lax.fori_loop(1, 32, spread_arrive, 0)

    g_copies = []
    for k in (0, 1):
        slot = 2 * k + core
        copy = remote(gram.at[slot], gram.at[slot], send_g.at[k], recv_g.at[slot], core=1 - core)
        copy.start()
        g_copies.append(copy)
    for k in (0, 1):
        slot = 2 * k + 1 - core
        arrived(gram.at[slot], recv_g.at[slot])

    arrived(left.at[1 - yl], recv_one.at[1])
    arrived(theirs, recv_one.at[3])

    @pl.when(has_columns)
    def _():
        kept_copy.wait_send()

    def drain(step, _):
        scatter_copy(step).wait_send()
        spread_copy(step, 1).wait_send()
        spread_copy(step, 0).wait_send()
        return 0

    lax.fori_loop(1, 32, drain, 0)
    spread_copy(0, 1).wait_send()
    for copy in sq_copies + core_copies + [y_copy, left_copy, right_copy] + w_copies + g_copies:
        copy.wait_send()
    for copy in waits:
        copy.wait_send()

    @pl.when(yl != yh)
    def _():
        for h in (0, 1):
            for n, (src, dst) in enumerate(pieces_of(h)):
                lend_copy(h, n, src, dst).wait_send()


def gather_and_power(gradient, basis, left_old):
    any_space = pl.BlockSpec(memory_space=pl.ANY)
    vmem = pl.BlockSpec(memory_space=pltpu.VMEM)
    dma = pltpu.SemaphoreType.DMA
    f32, bf16 = jnp.float32, jnp.bfloat16
    return pl.pallas_call(
        main_kernel,
        out_shape=(
            jax.ShapeDtypeStruct((4, 32, 8, 256), f32),
            jax.ShapeDtypeStruct((4, 80, 128), f32),
            jax.ShapeDtypeStruct((2, 80, 320), f32),
            jax.ShapeDtypeStruct((4, 8, 128), f32),
            jax.ShapeDtypeStruct((80, 640), f32),
            jax.ShapeDtypeStruct((80, 640), f32),
        ),
        in_specs=[any_space] * 3,
        out_specs=(vmem,) * 6,
        scratch_shapes=[
            pltpu.VMEM((2, 2, 4, 320, 384), bf16),
            pltpu.VMEM((2, 80, 640), bf16),
            pltpu.VMEM((4, 80, 384), f32),
            pltpu.VMEM((8, 128), f32),
            pltpu.VMEM((4, 80, 320), bf16),
            pltpu.VMEM((80, 640), f32),
            pltpu.VMEM((4, 80, 320), f32),
            pltpu.VMEM((4, 80, 320), f32),
            pltpu.VMEM((4, 80, 320), f32),
            pltpu.VMEM((2, 80, 128), f32),
            pltpu.VMEM((2, 80, 128), f32),
            pltpu.VMEM((32, 8, 256), f32),
            pltpu.VMEM((32, 8, 256), f32),
            dma((2, 3)), dma((2, 2, 16)), dma((64,)), dma((4,)), dma((1,)), dma((4,)), dma((2,)),
            dma((4,)), dma((4,)),
            dma((3,)), dma((4,)),
            dma((2,)), dma((4,)),
            dma((4,)), dma((4,)),
            dma((32,)), dma((32,)),
            dma((2, 32)), dma((2, 32)),
            dma((2,)), dma((4,)),
        ],
        compiler_params=pltpu.CompilerParams(
            collective_id=0, has_side_effects=True, vmem_limit_bytes=48 << 20
        ),
    )(gradient, basis, left_old)


def eliminate(block):
    n = 128
    sub = lax.broadcasted_iota(jnp.int32, (8, n), 0)
    lane = lax.broadcasted_iota(jnp.int32, (8, n), 1)
    m = [block[at : at + 8, :] for at in range(0, n, 8)]
    for b in range(n // 8):
        at = 8 * b
        inside = (lane >= at) & (lane < at + 8)

        def columns_of(v):
            return [jnp.broadcast_to(v[:, at + j : at + j + 1], (8, n)) for j in range(8)]

        rows = m[b]
        cols = columns_of(rows)
        rows = jnp.where(inside, (lane - at == sub).astype(jnp.float32), rows)
        more = b + 1 < n // 8
        if more:
            next_rows = m[b + 1]
            next_cols = columns_of(next_rows)
            next_rows = jnp.where(inside, 0.0, next_rows)
        for j in range(8):
            scale = lax.rsqrt(jnp.broadcast_to(cols[j][j : j + 1, :], (8, n)))
            below = jnp.where(sub > j, cols[j] * scale, 0.0)
            pivot = jnp.broadcast_to(rows[j : j + 1, :], (8, n)) * scale
            rows = jnp.where(sub == j, pivot, rows - below * pivot)
            if more:
                next_below = next_cols[j] * scale
                next_rows = next_rows - next_below * pivot
            for k in range(j + 1, 8):
                row = jnp.broadcast_to(cols[k][j : j + 1, :], (8, n)) * scale
                cols[k] = cols[k] - below * row
                if more:
                    next_cols[k] = next_cols[k] - next_below * row
        m[b] = rows
        if more:
            m[b + 1] = next_rows
        if b + 2 < n // 8:
            change = full_dot(rows, rows, TN)
            for i in range(b + 2, n // 8):
                m[i] = jnp.where(inside, 0.0, m[i]) - change[8 * i : 8 * i + 8, :]
    return jnp.concatenate(m, axis=0)


def factor_kernel(
    gram_ref, w_ref, left_ref, sq_ref, ours_ref, theirs_ref, right_old_ref,
    left_stat_ref, right_stat_ref, q_ref, m_ref,
):
    order = 512
    n = 128
    role = 2 * lax.axis_index("yl") + lax.axis_index("core")
    weight = stat_weight(jnp.sum(sq_ref[0] + sq_ref[1] + sq_ref[2] + sq_ref[3]))[:1, :1]
    left_stat_ref[:, :320] = left_ref[0]
    left_stat_ref[:, 320:] = left_ref[1]
    right_stat_ref[...] = smoothing * right_old_ref[...] + weight * (ours_ref[...] + theirs_ref[...])
    for r in range(4):
        for t in range(16):
            for pair in (0, 1):
                at = n * r + 8 * t
                m_ref[at : at + 8, 256 * pair : 256 * pair + 256] = gram_ref[r, 2 * t + pair]
        m_ref[order:, n * r : n * r + n] = w_ref[r]
    row = lax.broadcasted_iota(jnp.int32, (n, n), 0)
    col = lax.broadcasted_iota(jnp.int32, (n, n), 1)
    for at in range(0, order, n):
        end = at + n
        inverse = jnp.where(col <= row, eliminate(m_ref[at:end, at:end]), 0.0)
        panel = full_dot(m_ref[end:, at:end], inverse, NT)

        @pl.when(role == at // n)
        def _():
            q_ref[...] = panel[order - end :, :]

        if end < order:
            m_ref[end:, end:] = m_ref[end:, end:] - full_dot(panel, panel[: order - end, :], NT)


def factor(gram, power, left, squares, ours, theirs, right_old):
    return pl.pallas_call(
        factor_kernel,
        out_shape=(
            jax.ShapeDtypeStruct((80, 640), jnp.float32),
            jax.ShapeDtypeStruct((80, 640), jnp.float32),
            jax.ShapeDtypeStruct((80, 128), jnp.float32),
        ),
        in_specs=[pl.BlockSpec(memory_space=pltpu.VMEM)] * 7,
        out_specs=(pl.BlockSpec(memory_space=pltpu.VMEM),) * 3,
        scratch_shapes=[pltpu.VMEM((592, 512), jnp.float32)],
        compiler_params=pltpu.CompilerParams(vmem_limit_bytes=32 << 20),
    )(gram, power, left, squares, ours, theirs, right_old)


def on_device(gradient, left_old, right_old, basis_old):
    gathered = gather_and_power(gradient, basis_old, left_old)
    return factor(*gathered, right_old)


def solution(mesh):
    finer = Mesh(mesh.devices.reshape(2, 2, 4, 2, 4), ("yl", "core", "z", "yh", "x"))
    return jax.shard_map(
        on_device,
        mesh=finer,
        in_specs=(P(SHARD, ROLE),) * 4,
        out_specs=(P(SHARD, ROLE),) * 3,
        check_vma=False,
    )
```

```python
import jax
import jax.numpy as jnp
from jax import lax
from jax.experimental import pallas as pl
from jax.experimental.pallas import tpu as pltpu
from jax.sharding import Mesh
from jax.sharding import PartitionSpec as P

SHARD = ("z", "yh", "x")
ROLE = ("yl", "core")
MESH = pl.DeviceIdType.MESH

smoothing = 0.95
clip_ratio = 4.0
epsilon_value = 1e-06

NN = (((1,), (0,)), ((), ()))
TN = (((0,), (0,)), ((), ()))
NT = (((1,), (1,)), ((), ()))


def bf16_dot(a, b, dims):
    return lax.dot_general(a, b, dims, preferred_element_type=jnp.float32)


def remote(src, dst, send_sem, recv_sem, **target):
    return pltpu.make_async_remote_copy(
        src_ref=src,
        dst_ref=dst,
        send_sem=send_sem,
        recv_sem=recv_sem,
        device_id=target,
        device_id_type=MESH,
    )


def arrived(ref, sem):
    pltpu.make_async_copy(ref, ref, sem).wait()


def ring(axis, step):
    return lax.rem(lax.axis_index(axis) + (4 + step), 4)


def greet(barrier, **target):
    pl.semaphore_signal(barrier, inc=1, device_id=target, device_id_type=MESH)


def stat_weight(squares):
    full = jnp.full((8, 128), squares + epsilon_value, jnp.float32)
    factor = jnp.minimum(1.0, clip_ratio * jnp.sqrt(jnp.float32(2560)) / jnp.sqrt(full))
    return (1.0 - smoothing) * (factor * factor)


def parts_of(x):
    high = x.astype(jnp.bfloat16)
    rest = x - high.astype(jnp.float32)
    middle = rest.astype(jnp.bfloat16)
    low = (rest - middle.astype(jnp.float32)).astype(jnp.bfloat16)
    return high, middle, low


def full_dot(a, b, dims):
    a_axis, b_axis = dims[0][0][0], dims[0][1][0]
    ah, am, al = parts_of(a)
    bh, bm, bl = (ah, am, al) if b is a else parts_of(b)
    left = jnp.concatenate([ah, ah, am, ah, al, am], axis=a_axis)
    right = jnp.concatenate([bh, bm, bh, bl, bh, bm], axis=b_axis)
    return bf16_dot(left, right, dims)


def main_kernel(
    gradient, basis, left_old,
    gram, power, left, squares, ours, theirs,
    blocks, mine, half, sq_sum, kept, right_out, partial, partial_in, stat, power_part, power_in, chunk, pieces,
    give, recv, send, send_y, recv_mine, recv_half, local_sem,
    send_core, recv_core, send_sq, recv_sq, send_w, recv_w, send_one, recv_one,
    send_rs, recv_rs, send_ag, recv_ag, send_g, recv_g,
):
    z, yh, x = (lax.axis_index(a) for a in SHARD)
    yl, core = (lax.axis_index(a) for a in ROLE)
    role = 2 * yl + core
    across = 2 * (1 - yl) + core
    shard = z * 8 + yh * 4 + x

    group = lax.rem(yl + yh, 2)
    strip_at = 2 * group + core
    strip_over = 2 * (1 - group) + core

    def peer(turn):
        at_z = lax.rem(z + 2 + turn // 8, 4)
        at_x = lax.rem(x + 2 + lax.rem(turn, 4), 4)
        at_yh = lax.rem(yh + 1 + lax.rem(turn // 4, 2), 2)
        at_yl = lax.rem(group + at_yh, 2)
        return at_z * 8 + at_yh * 4 + at_x, {"z": at_z, "yh": at_yh, "x": at_x, "yl": at_yl}

    def over_peers(body, init):
        return lax.fori_loop(23, 32, body, lax.fori_loop(0, 22, body, init))

    barrier = pltpu.get_barrier_semaphore()
    for dh, dl, dc in ((0, 0, 1), (0, 1, 0), (0, 1, 1), (1, 0, 0), (1, 1, 0)):
        greet(
            barrier,
            yh=lax.rem(yh + dh, 2),
            yl=lax.rem(yl + dl, 2),
            core=lax.rem(core + dc, 2),
        )
    for axis in ("z", "x"):
        for step in (1, -1):
            greet(barrier, **{axis: ring(axis, step)})

    own_rows = pltpu.make_async_copy(gradient, mine.at[yl], local_sem.at[0])
    own_rows.start()
    own_half = pltpu.make_async_copy(
        left_old.at[:, pl.ds(pl.multiple_of(256 * yl, 128), 384)], half.at[role], local_sem.at[1]
    )
    own_half.start()
    sq_sum[...] = jnp.zeros((8, 128), jnp.float32)
    waits = []

    pl.semaphore_wait(barrier, 9)

    def unit(h, k, at_z, at_x):
        return blocks.at[h, k, at_z, pl.ds(pl.multiple_of(at_x * 80, 16), 80), :]

    def sem(h, k, at_z, at_x):
        return recv.at[h, k, at_z * 4 + at_x]

    def pieces_of(h):
        to = unit(h, yl, z, x)
        if h == 0:
            return [(gradient.at[:, :384], to)]
        return [(gradient.at[:, 384:], to.at[:, :256]), (basis, to.at[:, 256:])]

    def give_copy(h, n, src, dst):
        return remote(src, dst, give.at[0, h + n], sem(h, yl, z, x), yh=1 - yh, yl=yh)

    def lend_copy(h, n, src, dst):
        return remote(src, dst, give.at[1, h + n], sem(h, yl, z, x), yl=yh)

    for h in (0, 1):
        for n, (src, dst) in enumerate(pieces_of(h)):
            copy = give_copy(h, n, src, dst)
            copy.start()
            waits.append(copy)

            @pl.when(yl == yh)
            def _():
                pltpu.make_async_copy(src, dst, sem(h, yl, z, x)).start()

            @pl.when(yl != yh)
            def _():
                lend_copy(h, n, src, dst).start()

    counter = [0]

    def push(h, k, at_z, at_x, axis, step):
        ref = unit(h, k, at_z, at_x)
        copy = remote(
            ref, ref, send.at[counter[0]], sem(h, k, at_z, at_x), **{axis: ring(axis, step)}
        )
        counter[0] += 1
        copy.start()
        waits.append(copy)

    def place(h, first, second):
        return (second, first) if h == 0 else (first, second)

    FIRST = ("x", "z")
    SECOND = ("z", "x")
    here = {"z": z, "x": x}

    def spread(h, k, onward, first, second):
        at_z, at_x = place(h, first, second)
        push(h, k, at_z, at_x, SECOND[h], onward)
        push(h, k, at_z, at_x, SECOND[h], -onward)

    def wait_unit(h, k, first, second):
        at_z, at_x = place(h, first, second)
        arrived(unit(h, k, at_z, at_x), sem(h, k, at_z, at_x))

    def add_squares(h, k, first, second):
        at_z, at_x = place(h, first, second)
        width = 384 if h == 0 else 256
        start = pl.multiple_of(at_x * 80, 16)
        value = blocks[h, k, at_z, pl.ds(start, 80), :width].astype(jnp.float32)
        value = value * value
        wide = value[:, :128]
        for lane in range(128, width, 128):
            wide = wide + value[:, lane : lane + 128]
        total = wide[:8]
        for row in range(8, 80, 8):
            total = total + wide[row : row + 8]
        sq_sum[...] += total

    def step_one(h, k, first, second, step):
        at_z, at_x = place(h, first, second)
        push(h, k, at_z, at_x, FIRST[h], step)

    both = [(k, h, onward) for k, onward in ((yh, 1), (1 - yh, -1)) for h in (0, 1)]

    for k, h, onward in both:
        wait_unit(h, k, here[FIRST[h]], here[SECOND[h]])
        step_one(h, k, here[FIRST[h]], here[SECOND[h]], onward)
        step_one(h, k, here[FIRST[h]], here[SECOND[h]], -onward)
    for toward in (1, -1):
        for k, h, onward in both:
            at_z, at_x = place(h, here[FIRST[h]], here[SECOND[h]])
            push(h, k, at_z, at_x, SECOND[h], toward * onward)
    to_partner = remote(gradient, mine.at[yl], send_y.at[0], recv_mine.at[0], yl=1 - yl)
    to_partner.start()
    waits.append(to_partner)
    to_core = remote(
        left_old.at[:, pl.ds(pl.multiple_of(256 * yl, 128), 384)],
        half.at[role],
        send_y.at[1],
        recv_half.at[role],
        core=1 - core,
    )
    to_core.start()
    waits.append(to_core)
    for k, h, onward in both:
        add_squares(h, k, here[FIRST[h]], here[SECOND[h]])
    for k, h, onward in both:
        behind = ring(FIRST[h], -onward)
        wait_unit(h, k, behind, here[SECOND[h]])
        step_one(h, k, behind, here[SECOND[h]], onward)
    for k, h, onward in both:
        spread(h, k, onward, ring(FIRST[h], -onward), here[SECOND[h]])
    for k, h, onward in both:
        ahead = ring(FIRST[h], onward)
        wait_unit(h, k, ahead, here[SECOND[h]])
        spread(h, k, onward, ahead, here[SECOND[h]])
    for k, h, onward in both:
        add_squares(h, k, ring(FIRST[h], -onward), here[SECOND[h]])
        add_squares(h, k, ring(FIRST[h], onward), here[SECOND[h]])
    for k, h, onward in both:
        far = ring(FIRST[h], 2)
        wait_unit(h, k, far, here[SECOND[h]])
        spread(h, k, onward, far, here[SECOND[h]])

    for dc in (0, 1):
        over = remote(
            left_old.at[:, pl.ds(pl.multiple_of(256 * (1 - yl), 128), 384)],
            half.at[role],
            send_y.at[2 + dc],
            recv_half.at[role],
            yl=1 - yl,
            core=lax.rem(core + dc, 2),
        )
        over.start()
        waits.append(over)
    for k, h, onward in both:
        add_squares(h, k, ring(FIRST[h], 2), here[SECOND[h]])

    def column(h, onward, turn):
        return ring(FIRST[h], (0, -onward, onward, 2)[turn])

    for turn in range(4):
        for k, h, onward in both:
            behind = ring(SECOND[h], -onward)
            first = column(h, onward, turn)
            wait_unit(h, k, first, behind)
            at_z, at_x = place(h, first, behind)
            push(h, k, at_z, at_x, SECOND[h], onward)
        for k, h, onward in both:
            add_squares(h, k, column(h, onward, turn), ring(SECOND[h], -onward))
    own_half.wait()
    for dl, dc in ((0, 1), (1, 0), (1, 1)):
        other = 2 * lax.rem(yl + dl, 2) + lax.rem(core + dc, 2)
        arrived(half.at[other], recv_half.at[other])
    for at_z in range(4):
        held = half[at_z]
        stat[at_z] = smoothing * jnp.where(yl == 0, held[:, :320], held[:, 64:])
    for turn in range(4):
        for k, h, onward in both:
            first = column(h, onward, turn)
            ahead, far = ring(SECOND[h], onward), ring(SECOND[h], 2)
            wait_unit(h, k, first, ahead)
            add_squares(h, k, first, ahead)
            wait_unit(h, k, first, far)
            add_squares(h, k, first, far)
    own_rows.wait()
    arrived(mine.at[1 - yl], recv_mine.at[0])

    squares[role] = sq_sum[...]
    sq_copies = []
    for n, (dl, dc) in enumerate(((1, 0), (0, 1), (1, 1))):
        copy = remote(
            squares.at[role],
            squares.at[role],
            send_sq.at[n],
            recv_sq.at[role],
            yl=lax.rem(yl + dl, 2),
            core=lax.rem(core + dc, 2),
        )
        copy.start()
        sq_copies.append(copy)
    core_copies = []
    for at_z in range(4):
        total = jnp.zeros((80, 320), jnp.float32)
        for k in (0, 1):
            total += bf16_dot(mine[k, :, :384], blocks[0, k, at_z], NT)
            total += bf16_dot(mine[k, :, 384:], blocks[1, k, at_z, :, :256], NT)
        partial[at_z] = total
        copy = remote(
            partial.at[at_z],
            partial_in.at[at_z],
            send_core.at[at_z],
            recv_core.at[at_z],
            core=1 - core,
        )
        copy.start()
        core_copies.append(copy)

    for dl, dc in ((0, 1), (1, 0), (1, 1)):
        other = 2 * lax.rem(yl + dl, 2) + lax.rem(core + dc, 2)
        arrived(squares.at[other], recv_sq.at[other])
    all_squares = jnp.sum(squares[0] + squares[1] + squares[2] + squares[3])
    weight = stat_weight(all_squares)[:1, :1]

    sums = [jnp.zeros((80, 128), jnp.float32)] * 2
    for at_z in range(4):
        core_copies[at_z].wait_recv()
        value = stat[at_z] + weight * (partial[at_z] + partial_in[at_z])
        stat[at_z] = value
        stacked = jnp.concatenate(parts_of(value), axis=0)
        for k in (0, 1):
            product = bf16_dot(stacked, blocks[1, k, at_z, :, 256:], NN)
            sums[k] = sums[k] + (product[:80] + product[80:160] + product[160:])
    for k in (0, 1):
        power_part[k] = sums[k]
    y_copy = remote(power_part, power_in, send_one.at[0], recv_one.at[0], yl=1 - yl)
    y_copy.start()
    left[yl] = stat[role]
    left_copy = remote(stat.at[across], left.at[yl], send_one.at[1], recv_one.at[1], yl=1 - yl)
    left_copy.start()

    has_columns = core == lax.rem(z, 2)
    kept_copy = remote(kept, kept, send_one.at[2], recv_one.at[2], core=1 - core)

    @pl.when(has_columns)
    def _():
        offset = 80 * (4 * yh + x)
        row = lax.broadcasted_iota(jnp.int32, (80, 640), 0)
        col = lax.broadcasted_iota(jnp.int32, (80, 640), 1)
        pick = jnp.where(col == row + offset, 1.0, 0.0).astype(jnp.bfloat16)
        for at_z in range(4):
            chosen = bf16_dot(pick[:, :384], blocks[0, z // 2, at_z], NT)
            chosen += bf16_dot(pick[:, 384:], blocks[1, z // 2, at_z, :, :256], NT)
            kept[at_z] = chosen.astype(jnp.bfloat16)
        kept_copy.start()

    y_copy.wait_recv()
    w_copies = []
    for k in (0, 1):
        slot = 2 * k + core
        power[slot] = power_part[k] + power_in[k]
        copy = remote(power.at[slot], power.at[slot], send_w.at[k], recv_w.at[slot], core=1 - core)
        copy.start()
        w_copies.append(copy)
    for k in (0, 1):
        slot = 2 * k + 1 - core
        arrived(power.at[slot], recv_w.at[slot])

    columns = power[strip_at]
    for pair in (0, 1):
        strip = full_dot(columns, jnp.concatenate([power[2 * pair], power[2 * pair + 1]], axis=1), TN)
        for t in range(16):
            chunk[2 * t + pair] = strip[8 * t : 8 * t + 8, :]

    def scatter_copy(turn):
        other, place = peer(turn)
        return remote(
            chunk.at[other], pieces.at[shard], send_rs.at[other], recv_rs.at[shard], **place
        )

    def scatter_start(turn, _):
        scatter_copy(turn).start()
        return 0

    over_peers(scatter_start, 0)

    @pl.when(jnp.logical_not(has_columns))
    def _():
        arrived(kept, recv_one.at[2])

    def right_product(k, out):
        for h, width in ((0, 384), (1, 256)):
            total = jnp.zeros((80, width), jnp.float32)
            for at_z in range(4):
                total += bf16_dot(kept[at_z], blocks[h, k, at_z, :, :width], NN)
            out[:, 384 * h : 384 * h + width] = total

    right_product(1 - yl, right_out)
    right_copy = remote(right_out, theirs, send_one.at[3], recv_one.at[3], yl=1 - yl)
    right_copy.start()

    def scatter_arrive(turn, total):
        other, _ = peer(turn)
        arrived(pieces.at[other], recv_rs.at[other])
        return total + pieces[other]

    gram[strip_at, shard] = over_peers(scatter_arrive, chunk[shard])

    def spread_copy(turn, flip):
        other, place = peer(turn)
        if flip:
            place = dict(place, yl=1 - place["yl"])
        return remote(
            gram.at[strip_at, shard],
            gram.at[strip_at, shard],
            send_ag.at[flip, other],
            recv_ag.at[flip, shard],
            **place,
        )

    def spread_start(turn, _):
        spread_copy(turn, 1).start()
        spread_copy(turn, 0).start()
        return 0

    over_peers(spread_start, 0)
    spread_copy(22, 1).start()
    right_product(yl, ours)

    def spread_arrive(turn, _):
        other, _ = peer(turn)
        arrived(gram.at[strip_over, other], recv_ag.at[1, other])
        arrived(gram.at[strip_at, other], recv_ag.at[0, other])
        return 0

    arrived(gram.at[strip_over, shard], recv_ag.at[1, shard])
    over_peers(spread_arrive, 0)

    g_copies = []
    for k in (0, 1):
        slot = 2 * k + core
        copy = remote(gram.at[slot], gram.at[slot], send_g.at[k], recv_g.at[slot], core=1 - core)
        copy.start()
        g_copies.append(copy)
    for k in (0, 1):
        slot = 2 * k + 1 - core
        arrived(gram.at[slot], recv_g.at[slot])

    arrived(left.at[1 - yl], recv_one.at[1])
    arrived(theirs, recv_one.at[3])

    @pl.when(has_columns)
    def _():
        kept_copy.wait_send()

    def drain(turn, _):
        scatter_copy(turn).wait_send()
        spread_copy(turn, 1).wait_send()
        spread_copy(turn, 0).wait_send()
        return 0

    over_peers(drain, 0)
    spread_copy(22, 1).wait_send()
    for copy in sq_copies + core_copies + [y_copy, left_copy, right_copy] + w_copies + g_copies:
        copy.wait_send()
    for copy in waits:
        copy.wait_send()

    @pl.when(yl != yh)
    def _():
        for h in (0, 1):
            for n, (src, dst) in enumerate(pieces_of(h)):
                lend_copy(h, n, src, dst).wait_send()


def gather_and_power(gradient, basis, left_old):
    any_space = pl.BlockSpec(memory_space=pl.ANY)
    vmem = pl.BlockSpec(memory_space=pltpu.VMEM)
    dma = pltpu.SemaphoreType.DMA
    f32, bf16 = jnp.float32, jnp.bfloat16
    return pl.pallas_call(
        main_kernel,
        out_shape=(
            jax.ShapeDtypeStruct((4, 32, 8, 256), f32),
            jax.ShapeDtypeStruct((4, 80, 128), f32),
            jax.ShapeDtypeStruct((2, 80, 320), f32),
            jax.ShapeDtypeStruct((4, 8, 128), f32),
            jax.ShapeDtypeStruct((80, 640), f32),
            jax.ShapeDtypeStruct((80, 640), f32),
        ),
        in_specs=[any_space] * 3,
        out_specs=(vmem,) * 6,
        scratch_shapes=[
            pltpu.VMEM((2, 2, 4, 320, 384), bf16),
            pltpu.VMEM((2, 80, 640), bf16),
            pltpu.VMEM((4, 80, 384), f32),
            pltpu.VMEM((8, 128), f32),
            pltpu.VMEM((4, 80, 320), bf16),
            pltpu.VMEM((80, 640), f32),
            pltpu.VMEM((4, 80, 320), f32),
            pltpu.VMEM((4, 80, 320), f32),
            pltpu.VMEM((4, 80, 320), f32),
            pltpu.VMEM((2, 80, 128), f32),
            pltpu.VMEM((2, 80, 128), f32),
            pltpu.VMEM((32, 8, 256), f32),
            pltpu.VMEM((32, 8, 256), f32),
            dma((2, 3)), dma((2, 2, 16)), dma((64,)), dma((4,)), dma((1,)), dma((4,)), dma((2,)),
            dma((4,)), dma((4,)),
            dma((3,)), dma((4,)),
            dma((2,)), dma((4,)),
            dma((4,)), dma((4,)),
            dma((32,)), dma((32,)),
            dma((2, 32)), dma((2, 32)),
            dma((2,)), dma((4,)),
        ],
        compiler_params=pltpu.CompilerParams(
            collective_id=0, has_side_effects=True, vmem_limit_bytes=48 << 20
        ),
    )(gradient, basis, left_old)


def eliminate(block):
    n = 128
    sub = lax.broadcasted_iota(jnp.int32, (8, n), 0)
    lane = lax.broadcasted_iota(jnp.int32, (8, n), 1)
    m = [block[at : at + 8, :] for at in range(0, n, 8)]

    def columns_of(v, at):
        return [jnp.broadcast_to(v[:, at + j : at + j + 1], (8, n)) for j in range(8)]

    def row_of(v, j):
        return jnp.broadcast_to(v[j : j + 1, :], (8, n))

    cols = columns_of(m[0], 0)
    for b in range(n // 8):
        at = 8 * b
        inside = (lane >= at) & (lane < at + 8)
        rows = m[b]
        more = b + 1 < n // 8
        if more:
            next_rows = m[b + 1]
            next_cols = columns_of(next_rows, at)
            later = columns_of(rows, at + 8)
            next_later = columns_of(next_rows, at + 8)
            next_rows = jnp.where(inside, 0.0, next_rows)
        rows = jnp.where(inside, (lane - at == sub).astype(jnp.float32), rows)
        for j in range(8):
            scale = lax.rsqrt(row_of(cols[j], j))
            below = jnp.where(sub > j, cols[j] * scale, 0.0)
            pivot = row_of(rows, j) * scale
            rows = jnp.where(sub == j, pivot, rows - below * pivot)
            if more:
                next_below = next_cols[j] * scale
                next_rows = next_rows - next_below * pivot
            for k in range(j + 1, 8):
                row = row_of(cols[k], j) * scale
                cols[k] = cols[k] - below * row
                if more:
                    next_cols[k] = next_cols[k] - next_below * row
            if more:
                for k in range(8):
                    row = row_of(later[k], j) * scale
                    later[k] = later[k] - below * row
                    next_later[k] = next_later[k] - next_below * row
        m[b] = rows
        if more:
            m[b + 1] = next_rows
            cols = next_later
        if b + 2 < n // 8:
            change = full_dot(rows, rows, TN)
            for i in range(b + 2, n // 8):
                m[i] = jnp.where(inside, 0.0, m[i]) - change[8 * i : 8 * i + 8, :]
    return jnp.concatenate(m, axis=0)


def factor_kernel(
    gram_ref, w_ref, left_ref, sq_ref, ours_ref, theirs_ref, right_old_ref,
    left_stat_ref, right_stat_ref, q_ref, m_ref,
):
    order = 512
    n = 128
    role = 2 * lax.axis_index("yl") + lax.axis_index("core")
    weight = stat_weight(jnp.sum(sq_ref[0] + sq_ref[1] + sq_ref[2] + sq_ref[3]))[:1, :1]
    left_stat_ref[:, :320] = left_ref[0]
    left_stat_ref[:, 320:] = left_ref[1]
    right_stat_ref[...] = smoothing * right_old_ref[...] + weight * (ours_ref[...] + theirs_ref[...])
    for r in range(4):
        for t in range(16):
            for pair in (0, 1):
                at = n * r + 8 * t
                m_ref[at : at + 8, 256 * pair : 256 * pair + 256] = gram_ref[r, 2 * t + pair]
        m_ref[order:, n * r : n * r + n] = w_ref[r]
    row = lax.broadcasted_iota(jnp.int32, (n, n), 0)
    col = lax.broadcasted_iota(jnp.int32, (n, n), 1)
    for at in range(0, order, n):
        end = at + n
        inverse = jnp.where(col <= row, eliminate(m_ref[at:end, at:end]), 0.0)
        panel = full_dot(m_ref[end:, at:end], inverse, NT)

        @pl.when(role == at // n)
        def _():
            q_ref[...] = panel[order - end :, :]

        if end < order:
            m_ref[end:, end:] = m_ref[end:, end:] - full_dot(panel, panel[: order - end, :], NT)


def factor(gram, power, left, squares, ours, theirs, right_old):
    return pl.pallas_call(
        factor_kernel,
        out_shape=(
            jax.ShapeDtypeStruct((80, 640), jnp.float32),
            jax.ShapeDtypeStruct((80, 640), jnp.float32),
            jax.ShapeDtypeStruct((80, 128), jnp.float32),
        ),
        in_specs=[pl.BlockSpec(memory_space=pltpu.VMEM)] * 7,
        out_specs=(pl.BlockSpec(memory_space=pltpu.VMEM),) * 3,
        scratch_shapes=[pltpu.VMEM((592, 512), jnp.float32)],
        compiler_params=pltpu.CompilerParams(vmem_limit_bytes=32 << 20),
    )(gram, power, left, squares, ours, theirs, right_old)


def on_device(gradient, left_old, right_old, basis_old):
    gathered = gather_and_power(gradient, basis_old, left_old)
    return factor(*gathered, right_old)


def solution(mesh):
    finer = Mesh(mesh.devices.reshape(2, 2, 4, 2, 4), ("yl", "core", "z", "yh", "x"))
    return jax.shard_map(
        on_device,
        mesh=finer,
        in_specs=(P(SHARD, ROLE),) * 4,
        out_specs=(P(SHARD, ROLE),) * 3,
        check_vma=False,
    )
```

```python
import jax
import jax.numpy as jnp
from jax import lax
from jax.experimental import pallas as pl
from jax.experimental.pallas import tpu as pltpu
from jax.sharding import Mesh
from jax.sharding import PartitionSpec as P

SHARD = ("z", "yh", "x")
ROLE = ("yl", "core")
MESH = pl.DeviceIdType.MESH

smoothing = 0.95
clip_ratio = 4.0
epsilon_value = 1e-06

NN = (((1,), (0,)), ((), ()))
TN = (((0,), (0,)), ((), ()))
NT = (((1,), (1,)), ((), ()))


def bf16_dot(a, b, dims):
    return lax.dot_general(a, b, dims, preferred_element_type=jnp.float32)


def remote(src, dst, send_sem, recv_sem, **target):
    return pltpu.make_async_remote_copy(
        src_ref=src,
        dst_ref=dst,
        send_sem=send_sem,
        recv_sem=recv_sem,
        device_id=target,
        device_id_type=MESH,
    )


def arrived(ref, sem):
    pltpu.make_async_copy(ref, ref, sem).wait()


def ring(axis, step):
    return lax.rem(lax.axis_index(axis) + (4 + step), 4)


def greet(barrier, **target):
    pl.semaphore_signal(barrier, inc=1, device_id=target, device_id_type=MESH)


def stat_weight(squares):
    full = jnp.full((8, 128), squares + epsilon_value, jnp.float32)
    factor = jnp.minimum(1.0, clip_ratio * jnp.sqrt(jnp.float32(2560)) / jnp.sqrt(full))
    return (1.0 - smoothing) * (factor * factor)


def parts_of(x):
    high = x.astype(jnp.bfloat16)
    rest = x - high.astype(jnp.float32)
    middle = rest.astype(jnp.bfloat16)
    low = (rest - middle.astype(jnp.float32)).astype(jnp.bfloat16)
    return high, middle, low


def full_dot(a, b, dims):
    a_axis, b_axis = dims[0][0][0], dims[0][1][0]
    ah, am, al = parts_of(a)
    bh, bm, bl = (ah, am, al) if b is a else parts_of(b)
    left = jnp.concatenate([ah, ah, am, ah, al, am], axis=a_axis)
    right = jnp.concatenate([bh, bm, bh, bl, bh, bm], axis=b_axis)
    return bf16_dot(left, right, dims)


def main_kernel(
    gradient, basis, left_old,
    gram, power, left, squares, ours, theirs,
    blocks, mine, half, sq_sum, kept, right_out, partial, partial_in, stat, power_part, power_in, chunk, pieces,
    give, recv, send, send_y, recv_mine, recv_half, local_sem,
    send_core, recv_core, send_sq, recv_sq, send_w, recv_w, send_one, recv_one,
    send_rs, recv_rs, send_ag, recv_ag, send_g, recv_g,
):
    z, yh, x = (lax.axis_index(a) for a in SHARD)
    yl, core = (lax.axis_index(a) for a in ROLE)
    role = 2 * yl + core
    across = 2 * (1 - yl) + core
    shard = z * 8 + yh * 4 + x

    group = lax.rem(yl + yh, 2)
    strip_at = 2 * group + core
    strip_over = 2 * (1 - group) + core

    def peer(turn):
        at_z = lax.rem(z + 2 + turn // 8, 4)
        at_x = lax.rem(x + 2 + lax.rem(turn, 4), 4)
        at_yh = lax.rem(yh + 1 + lax.rem(turn // 4, 2), 2)
        at_yl = lax.rem(group + at_yh, 2)
        return at_z * 8 + at_yh * 4 + at_x, {"z": at_z, "yh": at_yh, "x": at_x, "yl": at_yl}

    def over_peers(body, init):
        return lax.fori_loop(23, 32, body, lax.fori_loop(0, 22, body, init))

    barrier = pltpu.get_barrier_semaphore()
    for dh, dl, dc in ((0, 0, 1), (0, 1, 0), (0, 1, 1), (1, 0, 0), (1, 1, 0)):
        greet(
            barrier,
            yh=lax.rem(yh + dh, 2),
            yl=lax.rem(yl + dl, 2),
            core=lax.rem(core + dc, 2),
        )
    for axis in ("z", "x"):
        for step in (1, -1):
            greet(barrier, **{axis: ring(axis, step)})

    own_rows = pltpu.make_async_copy(gradient, mine.at[yl], local_sem.at[0])
    own_rows.start()
    own_half = pltpu.make_async_copy(
        left_old.at[:, pl.ds(pl.multiple_of(256 * yl, 128), 384)], half.at[role], local_sem.at[1]
    )
    own_half.start()
    sq_sum[...] = jnp.zeros((8, 128), jnp.float32)
    waits = []

    pl.semaphore_wait(barrier, 9)

    def unit(h, k, at_z, at_x):
        return blocks.at[h, k, at_z, pl.ds(pl.multiple_of(at_x * 80, 16), 80), :]

    def sem(h, k, at_z, at_x):
        return recv.at[h, k, at_z * 4 + at_x]

    def pieces_of(h):
        to = unit(h, yl, z, x)
        if h == 0:
            return [(gradient.at[:, :384], to)]
        return [(gradient.at[:, 384:], to.at[:, :256]), (basis, to.at[:, 256:])]

    def give_copy(h, n, src, dst):
        return remote(src, dst, give.at[0, h + n], sem(h, yl, z, x), yh=1 - yh, yl=yh)

    def lend_copy(h, n, src, dst):
        return remote(src, dst, give.at[1, h + n], sem(h, yl, z, x), yl=yh)

    for h in (0, 1):
        for n, (src, dst) in enumerate(pieces_of(h)):
            copy = give_copy(h, n, src, dst)
            copy.start()
            waits.append(copy)

            @pl.when(yl == yh)
            def _():
                pltpu.make_async_copy(src, dst, sem(h, yl, z, x)).start()

            @pl.when(yl != yh)
            def _():
                lend_copy(h, n, src, dst).start()

    counter = [0]

    def push(h, k, at_z, at_x, axis, step):
        ref = unit(h, k, at_z, at_x)
        copy = remote(
            ref, ref, send.at[counter[0]], sem(h, k, at_z, at_x), **{axis: ring(axis, step)}
        )
        counter[0] += 1
        copy.start()
        waits.append(copy)

    def place(h, first, second):
        return (second, first) if h == 0 else (first, second)

    FIRST = ("x", "z")
    SECOND = ("z", "x")
    here = {"z": z, "x": x}

    def spread(h, k, onward, first, second):
        at_z, at_x = place(h, first, second)
        push(h, k, at_z, at_x, SECOND[h], onward)
        push(h, k, at_z, at_x, SECOND[h], -onward)

    def wait_unit(h, k, first, second):
        at_z, at_x = place(h, first, second)
        arrived(unit(h, k, at_z, at_x), sem(h, k, at_z, at_x))

    def add_squares(h, k, first, second):
        at_z, at_x = place(h, first, second)
        width = 384 if h == 0 else 256
        start = pl.multiple_of(at_x * 80, 16)
        value = blocks[h, k, at_z, pl.ds(start, 80), :width].astype(jnp.float32)
        value = value * value
        wide = value[:, :128]
        for lane in range(128, width, 128):
            wide = wide + value[:, lane : lane + 128]
        total = wide[:8]
        for row in range(8, 80, 8):
            total = total + wide[row : row + 8]
        sq_sum[...] += total

    def step_one(h, k, first, second, step):
        at_z, at_x = place(h, first, second)
        push(h, k, at_z, at_x, FIRST[h], step)

    both = [(k, h, onward) for k, onward in ((yh, 1), (1 - yh, -1)) for h in (0, 1)]

    for k, h, onward in both:
        wait_unit(h, k, here[FIRST[h]], here[SECOND[h]])
        step_one(h, k, here[FIRST[h]], here[SECOND[h]], onward)
        step_one(h, k, here[FIRST[h]], here[SECOND[h]], -onward)
    for toward in (1, -1):
        for k, h, onward in both:
            at_z, at_x = place(h, here[FIRST[h]], here[SECOND[h]])
            push(h, k, at_z, at_x, SECOND[h], toward * onward)
    to_partner = remote(gradient, mine.at[yl], send_y.at[0], recv_mine.at[0], yl=1 - yl)
    to_partner.start()
    waits.append(to_partner)
    to_core = remote(
        left_old.at[:, pl.ds(pl.multiple_of(256 * yl, 128), 384)],
        half.at[role],
        send_y.at[1],
        recv_half.at[role],
        core=1 - core,
    )
    to_core.start()
    waits.append(to_core)
    for k, h, onward in both:
        add_squares(h, k, here[FIRST[h]], here[SECOND[h]])
    for k, h, onward in both:
        behind = ring(FIRST[h], -onward)
        wait_unit(h, k, behind, here[SECOND[h]])
        step_one(h, k, behind, here[SECOND[h]], onward)
    for k, h, onward in both:
        spread(h, k, onward, ring(FIRST[h], -onward), here[SECOND[h]])
    for k, h, onward in both:
        ahead = ring(FIRST[h], onward)
        wait_unit(h, k, ahead, here[SECOND[h]])
        spread(h, k, onward, ahead, here[SECOND[h]])
    for k, h, onward in both:
        add_squares(h, k, ring(FIRST[h], -onward), here[SECOND[h]])
        add_squares(h, k, ring(FIRST[h], onward), here[SECOND[h]])
    for k, h, onward in both:
        far = ring(FIRST[h], 2)
        wait_unit(h, k, far, here[SECOND[h]])
        spread(h, k, onward, far, here[SECOND[h]])

    for dc in (0, 1):
        over = remote(
            left_old.at[:, pl.ds(pl.multiple_of(256 * (1 - yl), 128), 384)],
            half.at[role],
            send_y.at[2 + dc],
            recv_half.at[role],
            yl=1 - yl,
            core=lax.rem(core + dc, 2),
        )
        over.start()
        waits.append(over)
    for k, h, onward in both:
        add_squares(h, k, ring(FIRST[h], 2), here[SECOND[h]])

    def column(h, onward, turn):
        return ring(FIRST[h], (0, -onward, onward, 2)[turn])

    for turn in range(4):
        for k, h, onward in both:
            behind = ring(SECOND[h], -onward)
            first = column(h, onward, turn)
            wait_unit(h, k, first, behind)
            at_z, at_x = place(h, first, behind)
            push(h, k, at_z, at_x, SECOND[h], onward)
        for k, h, onward in both:
            add_squares(h, k, column(h, onward, turn), ring(SECOND[h], -onward))
    own_half.wait()
    for dl, dc in ((0, 1), (1, 0), (1, 1)):
        other = 2 * lax.rem(yl + dl, 2) + lax.rem(core + dc, 2)
        arrived(half.at[other], recv_half.at[other])
    for at_z in range(4):
        held = half[at_z]
        stat[at_z] = smoothing * jnp.where(yl == 0, held[:, :320], held[:, 64:])
    for turn in range(4):
        for k, h, onward in both:
            first = column(h, onward, turn)
            ahead, far = ring(SECOND[h], onward), ring(SECOND[h], 2)
            wait_unit(h, k, first, ahead)
            add_squares(h, k, first, ahead)
            wait_unit(h, k, first, far)
            add_squares(h, k, first, far)
    own_rows.wait()
    arrived(mine.at[1 - yl], recv_mine.at[0])

    squares[role] = sq_sum[...]
    sq_copies = []
    for n, (dl, dc) in enumerate(((1, 0), (0, 1), (1, 1))):
        copy = remote(
            squares.at[role],
            squares.at[role],
            send_sq.at[n],
            recv_sq.at[role],
            yl=lax.rem(yl + dl, 2),
            core=lax.rem(core + dc, 2),
        )
        copy.start()
        sq_copies.append(copy)
    core_copies = []
    for at_z in range(4):
        total = jnp.zeros((80, 320), jnp.float32)
        for k in (0, 1):
            total += bf16_dot(mine[k, :, :384], blocks[0, k, at_z], NT)
            total += bf16_dot(mine[k, :, 384:], blocks[1, k, at_z, :, :256], NT)
        partial[at_z] = total
        copy = remote(
            partial.at[at_z],
            partial_in.at[at_z],
            send_core.at[at_z],
            recv_core.at[at_z],
            core=1 - core,
        )
        copy.start()
        core_copies.append(copy)

    for dl, dc in ((0, 1), (1, 0), (1, 1)):
        other = 2 * lax.rem(yl + dl, 2) + lax.rem(core + dc, 2)
        arrived(squares.at[other], recv_sq.at[other])
    all_squares = jnp.sum(squares[0] + squares[1] + squares[2] + squares[3])
    weight = stat_weight(all_squares)[:1, :1]

    sums = [jnp.zeros((80, 128), jnp.float32)] * 2
    for at_z in range(4):
        core_copies[at_z].wait_recv()
        value = stat[at_z] + weight * (partial[at_z] + partial_in[at_z])
        stat[at_z] = value
        stacked = jnp.concatenate(parts_of(value), axis=0)
        for k in (0, 1):
            product = bf16_dot(stacked, blocks[1, k, at_z, :, 256:], NN)
            sums[k] = sums[k] + (product[:80] + product[80:160] + product[160:])
    for k in (0, 1):
        power_part[k] = sums[k]
    y_copy = remote(power_part, power_in, send_one.at[0], recv_one.at[0], yl=1 - yl)
    y_copy.start()
    left[yl] = stat[role]
    left_copy = remote(stat.at[across], left.at[yl], send_one.at[1], recv_one.at[1], yl=1 - yl)
    left_copy.start()

    has_columns = core == lax.rem(z, 2)
    kept_copy = remote(kept, kept, send_one.at[2], recv_one.at[2], core=1 - core)

    @pl.when(has_columns)
    def _():
        offset = 80 * (4 * yh + x)
        row = lax.broadcasted_iota(jnp.int32, (80, 640), 0)
        col = lax.broadcasted_iota(jnp.int32, (80, 640), 1)
        pick = jnp.where(col == row + offset, 1.0, 0.0).astype(jnp.bfloat16)
        for at_z in range(4):
            chosen = bf16_dot(pick[:, :384], blocks[0, z // 2, at_z], NT)
            chosen += bf16_dot(pick[:, 384:], blocks[1, z // 2, at_z, :, :256], NT)
            kept[at_z] = chosen.astype(jnp.bfloat16)
        kept_copy.start()

    y_copy.wait_recv()
    w_copies = []
    for k in (0, 1):
        slot = 2 * k + core
        power[slot] = power_part[k] + power_in[k]
        copy = remote(power.at[slot], power.at[slot], send_w.at[k], recv_w.at[slot], core=1 - core)
        copy.start()
        w_copies.append(copy)
    for k in (0, 1):
        slot = 2 * k + 1 - core
        arrived(power.at[slot], recv_w.at[slot])

    def block(a, b):
        return full_dot(power[a], power[b], TN)

    half_row = lax.rem(strip_at, 2)
    thirds = (
        block(strip_at, strip_at),
        block(jnp.minimum(strip_at + 1, 3), lax.rem(strip_at, 3)),
        block(2 + half_row, half_row),
    )
    for n in (0, 1):
        for t in range(16):
            chunk[16 * n + t] = thirds[n][8 * t : 8 * t + 8]
    lower_half = jnp.where(strip_at < 2, thirds[2][:64], thirds[2][64:])
    for t in range(8):
        chunk[32 + t] = lower_half[8 * t : 8 * t + 8]
    doubled = shard < 8

    def scatter_copy(turn, more):
        other, place = peer(turn)
        return other, remote(
            chunk.at[32 * more + other],
            pieces.at[more, shard],
            send_rs.at[more, other],
            recv_rs.at[more, shard],
            **place,
        )

    def scatter_start(turn, _):
        other, copy = scatter_copy(turn, 0)
        copy.start()

        @pl.when(other < 8)
        def _():
            scatter_copy(turn, 1)[1].start()

        return 0

    over_peers(scatter_start, 0)

    @pl.when(jnp.logical_not(has_columns))
    def _():
        arrived(kept, recv_one.at[2])

    def right_product(k, out):
        for h, width in ((0, 384), (1, 256)):
            total = jnp.zeros((80, width), jnp.float32)
            for at_z in range(4):
                total += bf16_dot(kept[at_z], blocks[h, k, at_z, :, :width], NN)
            out[:, 384 * h : 384 * h + width] = total

    right_product(1 - yl, right_out)
    right_copy = remote(right_out, theirs, send_one.at[3], recv_one.at[3], yl=1 - yl)
    right_copy.start()

    def scatter_arrive(turn, total):
        other, _ = peer(turn)
        arrived(pieces.at[0, other], recv_rs.at[0, other])
        return total + pieces[0, other]

    def scatter_arrive_more(turn, total):
        other, _ = peer(turn)
        arrived(pieces.at[1, other], recv_rs.at[1, other])
        return total + pieces[1, other]

    def spread_copy(turn, flip, more):
        other, place = peer(turn)
        if flip:
            place = dict(place, yl=1 - place["yl"])
        tile = gram.at[strip_at, 32 * more + shard]
        return remote(
            tile, tile, send_ag.at[flip, more, other], recv_ag.at[flip, more, shard], **place
        )

    def spread_all(more):
        def spread_start(turn, _):
            spread_copy(turn, 1, more).start()
            spread_copy(turn, 0, more).start()
            return 0

        over_peers(spread_start, 0)
        spread_copy(22, 1, more).start()

    gram[strip_at, shard] = over_peers(scatter_arrive, chunk[shard])
    spread_all(0)

    @pl.when(doubled)
    def _():
        gram[strip_at, 32 + shard] = over_peers(scatter_arrive_more, chunk[32 + shard])
        spread_all(1)

    right_product(yl, ours)

    def tile_arrives(flip, other):
        strip = strip_over if flip else strip_at
        arrived(gram.at[strip, other], recv_ag.at[flip, 0, other])

        @pl.when(other < 8)
        def _():
            arrived(gram.at[strip, 32 + other], recv_ag.at[flip, 1, other])

    def spread_arrive(turn, _):
        other, _ = peer(turn)
        tile_arrives(1, other)
        tile_arrives(0, other)
        return 0

    tile_arrives(1, shard)
    over_peers(spread_arrive, 0)

    g_copies = []
    for k in (0, 1):
        slot = 2 * k + core
        copy = remote(gram.at[slot], gram.at[slot], send_g.at[k], recv_g.at[slot], core=1 - core)
        copy.start()
        g_copies.append(copy)
    for k in (0, 1):
        slot = 2 * k + 1 - core
        arrived(gram.at[slot], recv_g.at[slot])

    arrived(left.at[1 - yl], recv_one.at[1])
    arrived(theirs, recv_one.at[3])

    @pl.when(has_columns)
    def _():
        kept_copy.wait_send()

    def drain(turn, _):
        other, copy = scatter_copy(turn, 0)
        copy.wait_send()
        spread_copy(turn, 1, 0).wait_send()
        spread_copy(turn, 0, 0).wait_send()

        @pl.when(other < 8)
        def _():
            scatter_copy(turn, 1)[1].wait_send()

        @pl.when(doubled)
        def _():
            spread_copy(turn, 1, 1).wait_send()
            spread_copy(turn, 0, 1).wait_send()

        return 0

    over_peers(drain, 0)
    spread_copy(22, 1, 0).wait_send()

    @pl.when(doubled)
    def _():
        spread_copy(22, 1, 1).wait_send()

    for copy in sq_copies + core_copies + [y_copy, left_copy, right_copy] + w_copies + g_copies:
        copy.wait_send()
    for copy in waits:
        copy.wait_send()

    @pl.when(yl != yh)
    def _():
        for h in (0, 1):
            for n, (src, dst) in enumerate(pieces_of(h)):
                lend_copy(h, n, src, dst).wait_send()


def gather_and_power(gradient, basis, left_old):
    any_space = pl.BlockSpec(memory_space=pl.ANY)
    vmem = pl.BlockSpec(memory_space=pltpu.VMEM)
    dma = pltpu.SemaphoreType.DMA
    f32, bf16 = jnp.float32, jnp.bfloat16
    return pl.pallas_call(
        main_kernel,
        out_shape=(
            jax.ShapeDtypeStruct((4, 40, 8, 128), f32),
            jax.ShapeDtypeStruct((4, 80, 128), f32),
            jax.ShapeDtypeStruct((2, 80, 320), f32),
            jax.ShapeDtypeStruct((4, 8, 128), f32),
            jax.ShapeDtypeStruct((80, 640), f32),
            jax.ShapeDtypeStruct((80, 640), f32),
        ),
        in_specs=[any_space] * 3,
        out_specs=(vmem,) * 6,
        scratch_shapes=[
            pltpu.VMEM((2, 2, 4, 320, 384), bf16),
            pltpu.VMEM((2, 80, 640), bf16),
            pltpu.VMEM((4, 80, 384), f32),
            pltpu.VMEM((8, 128), f32),
            pltpu.VMEM((4, 80, 320), bf16),
            pltpu.VMEM((80, 640), f32),
            pltpu.VMEM((4, 80, 320), f32),
            pltpu.VMEM((4, 80, 320), f32),
            pltpu.VMEM((4, 80, 320), f32),
            pltpu.VMEM((2, 80, 128), f32),
            pltpu.VMEM((2, 80, 128), f32),
            pltpu.VMEM((40, 8, 128), f32),
            pltpu.VMEM((2, 32, 8, 128), f32),
            dma((2, 3)), dma((2, 2, 16)), dma((64,)), dma((4,)), dma((1,)), dma((4,)), dma((2,)),
            dma((4,)), dma((4,)),
            dma((3,)), dma((4,)),
            dma((2,)), dma((4,)),
            dma((4,)), dma((4,)),
            dma((2, 32)), dma((2, 32)),
            dma((2, 2, 32)), dma((2, 2, 32)),
            dma((2,)), dma((4,)),
        ],
        compiler_params=pltpu.CompilerParams(
            collective_id=0, has_side_effects=True, vmem_limit_bytes=48 << 20
        ),
    )(gradient, basis, left_old)


def eliminate(block):
    n = 128
    sub = lax.broadcasted_iota(jnp.int32, (8, n), 0)
    lane = lax.broadcasted_iota(jnp.int32, (8, n), 1)
    m = [block[at : at + 8, :] for at in range(0, n, 8)]

    def columns_of(v, at):
        return [jnp.broadcast_to(v[:, at + j : at + j + 1], (8, n)) for j in range(8)]

    def row_of(v, j):
        return jnp.broadcast_to(v[j : j + 1, :], (8, n))

    cols = columns_of(m[0], 0)
    for b in range(n // 8):
        at = 8 * b
        inside = (lane >= at) & (lane < at + 8)
        rows = m[b]
        ahead = list(range(b + 1, min(b + 3, n // 8)))
        ahead_cols = {i: columns_of(m[i], at) for i in ahead}
        if ahead:
            later = columns_of(rows, at + 8)
            next_later = columns_of(m[b + 1], at + 8)
        ahead_rows = {i: jnp.where(inside, 0.0, m[i]) for i in ahead}
        rows = jnp.where(inside, (lane - at == sub).astype(jnp.float32), rows)
        for j in range(8):
            scale = lax.rsqrt(row_of(cols[j], j))
            below = jnp.where(sub > j, cols[j] * scale, 0.0)
            pivot = row_of(rows, j) * scale
            rows = jnp.where(sub == j, pivot, rows - below * pivot)
            ahead_below = {i: ahead_cols[i][j] * scale for i in ahead}
            for i in ahead:
                ahead_rows[i] = ahead_rows[i] - ahead_below[i] * pivot
            for k in range(j + 1, 8):
                row = row_of(cols[k], j) * scale
                cols[k] = cols[k] - below * row
                for i in ahead:
                    ahead_cols[i][k] = ahead_cols[i][k] - ahead_below[i] * row
            if ahead:
                for k in range(8):
                    row = row_of(later[k], j) * scale
                    later[k] = later[k] - below * row
                    next_later[k] = next_later[k] - ahead_below[b + 1] * row
        m[b] = rows
        for i in ahead:
            m[i] = ahead_rows[i]
        if ahead:
            cols = next_later
        if b + 3 < n // 8:
            change = full_dot(rows, rows, TN)
            for i in range(b + 3, n // 8):
                m[i] = jnp.where(inside, 0.0, m[i]) - change[8 * i : 8 * i + 8, :]
    return jnp.concatenate(m, axis=0)


def factor_kernel(
    gram_ref, w_ref, left_ref, sq_ref, ours_ref, theirs_ref, right_old_ref,
    left_stat_ref, right_stat_ref, q_ref, m_ref,
):
    order = 512
    n = 128
    role = 2 * lax.axis_index("yl") + lax.axis_index("core")
    weight = stat_weight(jnp.sum(sq_ref[0] + sq_ref[1] + sq_ref[2] + sq_ref[3]))[:1, :1]
    left_stat_ref[:, :320] = left_ref[0]
    left_stat_ref[:, 320:] = left_ref[1]
    right_stat_ref[...] = smoothing * right_old_ref[...] + weight * (ours_ref[...] + theirs_ref[...])
    for r in range(4):
        below, half_row = min(r + 1, 3), r % 2
        for t in range(16):
            at = n * r + 8 * t
            m_ref[at : at + 8, n * r : n * r + n] = gram_ref[r, t]
            at = n * below + 8 * t
            m_ref[at : at + 8, n * (r % 3) : n * (r % 3) + n] = gram_ref[r, 16 + t]
        for t in range(8):
            at = n * (2 + half_row) + 64 * (r // 2) + 8 * t
            m_ref[at : at + 8, n * half_row : n * half_row + n] = gram_ref[r, 32 + t]
        m_ref[order:, n * r : n * r + n] = w_ref[r]
    row = lax.broadcasted_iota(jnp.int32, (n, n), 0)
    col = lax.broadcasted_iota(jnp.int32, (n, n), 1)
    for at in range(0, order, n):
        end = at + n
        inverse = jnp.where(col <= row, eliminate(m_ref[at:end, at:end]), 0.0)
        panel = full_dot(m_ref[end:, at:end], inverse, NT)

        @pl.when(role == at // n)
        def _():
            q_ref[...] = panel[order - end :, :]

        for to in range(end, order, n):
            change = full_dot(panel[to - end :, :], panel[to - end : to - end + n, :], NT)
            m_ref[to:, to : to + n] = m_ref[to:, to : to + n] - change


def factor(gram, power, left, squares, ours, theirs, right_old):
    return pl.pallas_call(
        factor_kernel,
        out_shape=(
            jax.ShapeDtypeStruct((80, 640), jnp.float32),
            jax.ShapeDtypeStruct((80, 640), jnp.float32),
            jax.ShapeDtypeStruct((80, 128), jnp.float32),
        ),
        in_specs=[pl.BlockSpec(memory_space=pltpu.VMEM)] * 7,
        out_specs=(pl.BlockSpec(memory_space=pltpu.VMEM),) * 3,
        scratch_shapes=[pltpu.VMEM((592, 512), jnp.float32)],
        compiler_params=pltpu.CompilerParams(vmem_limit_bytes=32 << 20),
    )(gram, power, left, squares, ours, theirs, right_old)


def on_device(gradient, left_old, right_old, basis_old):
    gathered = gather_and_power(gradient, basis_old, left_old)
    return factor(*gathered, right_old)


def solution(mesh):
    finer = Mesh(mesh.devices.reshape(2, 2, 4, 2, 4), ("yl", "core", "z", "yh", "x"))
    return jax.shard_map(
        on_device,
        mesh=finer,
        in_specs=(P(SHARD, ROLE),) * 4,
        out_specs=(P(SHARD, ROLE),) * 3,
        check_vma=False,
    )
```

```python
import jax
import jax.numpy as jnp
from jax import lax
from jax.experimental import pallas as pl
from jax.experimental.pallas import tpu as pltpu
from jax.sharding import Mesh
from jax.sharding import PartitionSpec as P

SHARD = ("z", "yh", "x")
ROLE = ("yl", "core")
MESH = pl.DeviceIdType.MESH

smoothing = 0.95
clip_ratio = 4.0
epsilon_value = 1e-06

NN = (((1,), (0,)), ((), ()))
TN = (((0,), (0,)), ((), ()))
NT = (((1,), (1,)), ((), ()))


def bf16_dot(a, b, dims):
    return lax.dot_general(a, b, dims, preferred_element_type=jnp.float32)


def remote(src, dst, send_sem, recv_sem, **target):
    return pltpu.make_async_remote_copy(
        src_ref=src,
        dst_ref=dst,
        send_sem=send_sem,
        recv_sem=recv_sem,
        device_id=target,
        device_id_type=MESH,
    )


def arrived(ref, sem):
    pltpu.make_async_copy(ref, ref, sem).wait()


def ring(axis, step):
    return lax.rem(lax.axis_index(axis) + (4 + step), 4)


def greet(barrier, **target):
    pl.semaphore_signal(barrier, inc=1, device_id=target, device_id_type=MESH)


def stat_weight(squares):
    full = jnp.full((8, 128), squares + epsilon_value, jnp.float32)
    factor = jnp.minimum(1.0, clip_ratio * jnp.sqrt(jnp.float32(2560)) / jnp.sqrt(full))
    return (1.0 - smoothing) * (factor * factor)


def parts_of(x):
    high = x.astype(jnp.bfloat16)
    rest = x - high.astype(jnp.float32)
    middle = rest.astype(jnp.bfloat16)
    low = (rest - middle.astype(jnp.float32)).astype(jnp.bfloat16)
    return high, middle, low


def full_dot(a, b, dims):
    a_axis, b_axis = dims[0][0][0], dims[0][1][0]
    ah, am, al = parts_of(a)
    bh, bm, bl = (ah, am, al) if b is a else parts_of(b)
    left = jnp.concatenate([ah, ah, am, ah, al, am], axis=a_axis)
    right = jnp.concatenate([bh, bm, bh, bl, bh, bm], axis=b_axis)
    return bf16_dot(left, right, dims)


def main_kernel(
    gradient, basis, left_old,
    gram, power, left, squares, ours, theirs,
    blocks, mine, half, sq_sum, kept, right_out, partial, partial_in, stat, power_part, power_in, chunk, pieces,
    give, recv, send, send_y, recv_mine, recv_half, local_sem,
    send_core, recv_core, send_sq, recv_sq, send_w, recv_w, send_one, recv_one,
    send_rs, recv_rs, send_ag, recv_ag, send_g, recv_g,
):
    z, yh, x = (lax.axis_index(a) for a in SHARD)
    yl, core = (lax.axis_index(a) for a in ROLE)
    role = 2 * yl + core
    across = 2 * (1 - yl) + core
    shard = z * 8 + yh * 4 + x

    group = lax.rem(yl + yh, 2)
    strip_at = 2 * group + core
    strip_over = 2 * (1 - group) + core

    def peer(turn):
        at_z = lax.rem(z + 2 + turn // 8, 4)
        at_x = lax.rem(x + 2 + lax.rem(turn, 4), 4)
        at_yh = lax.rem(yh + 1 + lax.rem(turn // 4, 2), 2)
        at_yl = lax.rem(group + at_yh, 2)
        return at_z * 8 + at_yh * 4 + at_x, {"z": at_z, "yh": at_yh, "x": at_x, "yl": at_yl}

    def owner(place):
        return 5 * place["z"] + place["x"] + place["yh"]

    def owns(place):
        upper, low = place["yh"] == 1, place["x"] < 2
        return jnp.logical_or(
            jnp.logical_and(jnp.logical_not(upper), place["x"] < 3),
            jnp.logical_and(upper, jnp.logical_not(low)),
        )

    own_place = {"z": z, "yh": yh, "x": x}

    def over_peers(body, init):
        return lax.fori_loop(23, 32, body, lax.fori_loop(0, 22, body, init))

    barrier = pltpu.get_barrier_semaphore()
    for dh, dl, dc in ((0, 0, 1), (0, 1, 0), (0, 1, 1), (1, 0, 0), (1, 1, 0)):
        greet(
            barrier,
            yh=lax.rem(yh + dh, 2),
            yl=lax.rem(yl + dl, 2),
            core=lax.rem(core + dc, 2),
        )
    for axis in ("z", "x"):
        for step in (1, -1):
            greet(barrier, **{axis: ring(axis, step)})

    own_rows = pltpu.make_async_copy(gradient, mine.at[yl], local_sem.at[0])
    own_rows.start()
    own_half = pltpu.make_async_copy(
        left_old.at[:, pl.ds(pl.multiple_of(256 * yl, 128), 384)], half.at[role], local_sem.at[1]
    )
    own_half.start()
    sq_sum[...] = jnp.zeros((8, 128), jnp.float32)
    waits = []

    pl.semaphore_wait(barrier, 9)

    def unit(h, k, at_z, at_x):
        return blocks.at[h, k, at_z, pl.ds(pl.multiple_of(at_x * 80, 16), 80), :]

    def sem(h, k, at_z, at_x):
        return recv.at[h, k, at_z * 4 + at_x]

    def pieces_of(h):
        to = unit(h, yl, z, x)
        if h == 0:
            return [(gradient.at[:, :384], to)]
        return [(gradient.at[:, 384:], to.at[:, :256]), (basis, to.at[:, 256:])]

    def give_copy(h, n, src, dst):
        return remote(src, dst, give.at[0, h + n], sem(h, yl, z, x), yh=1 - yh, yl=yh)

    def lend_copy(h, n, src, dst):
        return remote(src, dst, give.at[1, h + n], sem(h, yl, z, x), yl=yh)

    for h in (0, 1):
        for n, (src, dst) in enumerate(pieces_of(h)):
            copy = give_copy(h, n, src, dst)
            copy.start()
            waits.append(copy)

            @pl.when(yl == yh)
            def _():
                pltpu.make_async_copy(src, dst, sem(h, yl, z, x)).start()

            @pl.when(yl != yh)
            def _():
                lend_copy(h, n, src, dst).start()

    counter = [0]

    def push(h, k, at_z, at_x, axis, step):
        ref = unit(h, k, at_z, at_x)
        copy = remote(
            ref, ref, send.at[counter[0]], sem(h, k, at_z, at_x), **{axis: ring(axis, step)}
        )
        counter[0] += 1
        copy.start()
        waits.append(copy)

    def place(h, first, second):
        return (second, first) if h == 0 else (first, second)

    FIRST = ("x", "z")
    SECOND = ("z", "x")
    here = {"z": z, "x": x}

    def spread(h, k, onward, first, second):
        at_z, at_x = place(h, first, second)
        push(h, k, at_z, at_x, SECOND[h], onward)
        push(h, k, at_z, at_x, SECOND[h], -onward)

    def wait_unit(h, k, first, second):
        at_z, at_x = place(h, first, second)
        arrived(unit(h, k, at_z, at_x), sem(h, k, at_z, at_x))

    def add_squares(h, k, first, second):
        at_z, at_x = place(h, first, second)
        width = 384 if h == 0 else 256
        start = pl.multiple_of(at_x * 80, 16)
        value = blocks[h, k, at_z, pl.ds(start, 80), :width].astype(jnp.float32)
        value = value * value
        wide = value[:, :128]
        for lane in range(128, width, 128):
            wide = wide + value[:, lane : lane + 128]
        total = wide[:8]
        for row in range(8, 80, 8):
            total = total + wide[row : row + 8]
        sq_sum[...] += total

    def step_one(h, k, first, second, step):
        at_z, at_x = place(h, first, second)
        push(h, k, at_z, at_x, FIRST[h], step)

    both = [(k, h, onward) for k, onward in ((yh, 1), (1 - yh, -1)) for h in (0, 1)]

    for k, h, onward in both:
        wait_unit(h, k, here[FIRST[h]], here[SECOND[h]])
        step_one(h, k, here[FIRST[h]], here[SECOND[h]], onward)
        step_one(h, k, here[FIRST[h]], here[SECOND[h]], -onward)
    for toward in (1, -1):
        for k, h, onward in both:
            at_z, at_x = place(h, here[FIRST[h]], here[SECOND[h]])
            push(h, k, at_z, at_x, SECOND[h], toward * onward)
    to_partner = remote(gradient, mine.at[yl], send_y.at[0], recv_mine.at[0], yl=1 - yl)
    to_partner.start()
    waits.append(to_partner)
    to_core = remote(
        left_old.at[:, pl.ds(pl.multiple_of(256 * yl, 128), 384)],
        half.at[role],
        send_y.at[1],
        recv_half.at[role],
        core=1 - core,
    )
    to_core.start()
    waits.append(to_core)
    for k, h, onward in both:
        add_squares(h, k, here[FIRST[h]], here[SECOND[h]])
    for k, h, onward in both:
        behind = ring(FIRST[h], -onward)
        wait_unit(h, k, behind, here[SECOND[h]])
        step_one(h, k, behind, here[SECOND[h]], onward)
    for k, h, onward in both:
        spread(h, k, onward, ring(FIRST[h], -onward), here[SECOND[h]])
    for k, h, onward in both:
        ahead = ring(FIRST[h], onward)
        wait_unit(h, k, ahead, here[SECOND[h]])
        spread(h, k, onward, ahead, here[SECOND[h]])
    for k, h, onward in both:
        add_squares(h, k, ring(FIRST[h], -onward), here[SECOND[h]])
        add_squares(h, k, ring(FIRST[h], onward), here[SECOND[h]])
    for k, h, onward in both:
        far = ring(FIRST[h], 2)
        wait_unit(h, k, far, here[SECOND[h]])
        spread(h, k, onward, far, here[SECOND[h]])

    for dc in (0, 1):
        over = remote(
            left_old.at[:, pl.ds(pl.multiple_of(256 * (1 - yl), 128), 384)],
            half.at[role],
            send_y.at[2 + dc],
            recv_half.at[role],
            yl=1 - yl,
            core=lax.rem(core + dc, 2),
        )
        over.start()
        waits.append(over)
    for k, h, onward in both:
        add_squares(h, k, ring(FIRST[h], 2), here[SECOND[h]])

    def column(h, onward, turn):
        return ring(FIRST[h], (0, -onward, onward, 2)[turn])

    for turn in range(4):
        for k, h, onward in both:
            behind = ring(SECOND[h], -onward)
            first = column(h, onward, turn)
            wait_unit(h, k, first, behind)
            at_z, at_x = place(h, first, behind)
            push(h, k, at_z, at_x, SECOND[h], onward)
        for k, h, onward in both:
            add_squares(h, k, column(h, onward, turn), ring(SECOND[h], -onward))
    own_half.wait()
    for dl, dc in ((0, 1), (1, 0), (1, 1)):
        other = 2 * lax.rem(yl + dl, 2) + lax.rem(core + dc, 2)
        arrived(half.at[other], recv_half.at[other])
    for at_z in range(4):
        held = half[at_z]
        stat[at_z] = smoothing * jnp.where(yl == 0, held[:, :320], held[:, 64:])
    for turn in range(4):
        for k, h, onward in both:
            first = column(h, onward, turn)
            ahead, far = ring(SECOND[h], onward), ring(SECOND[h], 2)
            wait_unit(h, k, first, ahead)
            add_squares(h, k, first, ahead)
            wait_unit(h, k, first, far)
            add_squares(h, k, first, far)
    own_rows.wait()
    arrived(mine.at[1 - yl], recv_mine.at[0])

    squares[role] = sq_sum[...]
    sq_copies = []
    for n, (dl, dc) in enumerate(((1, 0), (0, 1), (1, 1))):
        copy = remote(
            squares.at[role],
            squares.at[role],
            send_sq.at[n],
            recv_sq.at[role],
            yl=lax.rem(yl + dl, 2),
            core=lax.rem(core + dc, 2),
        )
        copy.start()
        sq_copies.append(copy)
    core_copies = []
    for at_z in range(4):
        total = jnp.zeros((80, 320), jnp.float32)
        for k in (0, 1):
            total += bf16_dot(mine[k, :, :384], blocks[0, k, at_z], NT)
            total += bf16_dot(mine[k, :, 384:], blocks[1, k, at_z, :, :256], NT)
        partial[at_z] = total
        copy = remote(
            partial.at[at_z],
            partial_in.at[at_z],
            send_core.at[at_z],
            recv_core.at[at_z],
            core=1 - core,
        )
        copy.start()
        core_copies.append(copy)

    for dl, dc in ((0, 1), (1, 0), (1, 1)):
        other = 2 * lax.rem(yl + dl, 2) + lax.rem(core + dc, 2)
        arrived(squares.at[other], recv_sq.at[other])
    all_squares = jnp.sum(squares[0] + squares[1] + squares[2] + squares[3])
    weight = stat_weight(all_squares)[:1, :1]

    sums = [jnp.zeros((80, 128), jnp.float32)] * 2
    for at_z in range(4):
        core_copies[at_z].wait_recv()
        value = stat[at_z] + weight * (partial[at_z] + partial_in[at_z])
        stat[at_z] = value
        stacked = jnp.concatenate(parts_of(value), axis=0)
        for k in (0, 1):
            product = bf16_dot(stacked, blocks[1, k, at_z, :, 256:], NN)
            sums[k] = sums[k] + (product[:80] + product[80:160] + product[160:])
    for k in (0, 1):
        power_part[k] = sums[k]
    y_copy = remote(power_part, power_in, send_one.at[0], recv_one.at[0], yl=1 - yl)
    y_copy.start()
    left[yl] = stat[role]
    left_copy = remote(stat.at[across], left.at[yl], send_one.at[1], recv_one.at[1], yl=1 - yl)
    left_copy.start()

    has_columns = core == lax.rem(z, 2)
    kept_copy = remote(kept, kept, send_one.at[2], recv_one.at[2], core=1 - core)

    @pl.when(has_columns)
    def _():
        offset = 80 * (4 * yh + x)
        row = lax.broadcasted_iota(jnp.int32, (80, 640), 0)
        col = lax.broadcasted_iota(jnp.int32, (80, 640), 1)
        pick = jnp.where(col == row + offset, 1.0, 0.0).astype(jnp.bfloat16)
        for at_z in range(4):
            chosen = bf16_dot(pick[:, :384], blocks[0, z // 2, at_z], NT)
            chosen += bf16_dot(pick[:, 384:], blocks[1, z // 2, at_z, :, :256], NT)
            kept[at_z] = chosen.astype(jnp.bfloat16)
        kept_copy.start()

    y_copy.wait_recv()
    w_copies = []
    for k in (0, 1):
        slot = 2 * k + core
        power[slot] = power_part[k] + power_in[k]
        copy = remote(power.at[slot], power.at[slot], send_w.at[k], recv_w.at[slot], core=1 - core)
        copy.start()
        w_copies.append(copy)
    for k in (0, 1):
        slot = 2 * k + 1 - core
        arrived(power.at[slot], recv_w.at[slot])

    def block(a, b):
        return full_dot(power[a], power[b], TN)

    half_row = lax.rem(strip_at, 2)
    thirds = (
        block(strip_at, strip_at),
        block(jnp.minimum(strip_at + 1, 3), lax.rem(strip_at, 3)),
        block(2 + half_row, half_row),
    )
    for n in (0, 1):
        for t in range(8):
            chunk[8 * n + t] = thirds[n][16 * t : 16 * t + 16]
    lower_half = jnp.where(strip_at < 2, thirds[2][:64], thirds[2][64:])
    for t in range(4):
        chunk[16 + t] = lower_half[16 * t : 16 * t + 16]

    def scatter_copy(turn):
        other, place = peer(turn)
        copy = remote(
            chunk.at[owner(place)],
            pieces.at[shard],
            send_rs.at[other],
            recv_rs.at[shard],
            **place,
        )
        return place, copy

    def scatter_start(turn, _):
        place, copy = scatter_copy(turn)

        @pl.when(owns(place))
        def _():
            copy.start()

        return 0

    over_peers(scatter_start, 0)

    @pl.when(jnp.logical_not(has_columns))
    def _():
        arrived(kept, recv_one.at[2])

    def right_product(k, out):
        for h, width in ((0, 384), (1, 256)):
            total = jnp.zeros((80, width), jnp.float32)
            for at_z in range(4):
                total += bf16_dot(kept[at_z], blocks[h, k, at_z, :, :width], NN)
            out[:, 384 * h : 384 * h + width] = total

    right_product(1 - yl, right_out)
    right_copy = remote(right_out, theirs, send_one.at[3], recv_one.at[3], yl=1 - yl)
    right_copy.start()

    def scatter_arrive(turn, total):
        other, _ = peer(turn)
        arrived(pieces.at[other], recv_rs.at[other])
        return total + pieces[other]

    def spread_copy(turn, flip):
        other, place = peer(turn)
        if flip:
            place = dict(place, yl=1 - place["yl"])
        pair = gram.at[strip_at, owner(own_place)]
        return remote(pair, pair, send_ag.at[flip, other], recv_ag.at[flip, shard], **place)

    def spread_start(turn, _):
        spread_copy(turn, 1).start()
        spread_copy(turn, 0).start()
        return 0

    @pl.when(owns(own_place))
    def _():
        gram[strip_at, owner(own_place)] = over_peers(scatter_arrive, chunk[owner(own_place)])
        over_peers(spread_start, 0)
        spread_copy(22, 1).start()

    right_product(yl, ours)

    def pair_arrives(flip, other, place):
        strip = strip_over if flip else strip_at

        @pl.when(owns(place))
        def _():
            arrived(gram.at[strip, owner(place)], recv_ag.at[flip, other])

    def spread_arrive(turn, _):
        other, place = peer(turn)
        pair_arrives(1, other, place)
        pair_arrives(0, other, place)
        return 0

    pair_arrives(1, shard, own_place)
    over_peers(spread_arrive, 0)

    g_copies = []
    for k in (0, 1):
        slot = 2 * k + core
        copy = remote(gram.at[slot], gram.at[slot], send_g.at[k], recv_g.at[slot], core=1 - core)
        copy.start()
        g_copies.append(copy)
    for k in (0, 1):
        slot = 2 * k + 1 - core
        arrived(gram.at[slot], recv_g.at[slot])

    arrived(left.at[1 - yl], recv_one.at[1])
    arrived(theirs, recv_one.at[3])

    @pl.when(has_columns)
    def _():
        kept_copy.wait_send()

    def drain(turn, _):
        place, copy = scatter_copy(turn)

        @pl.when(owns(place))
        def _():
            copy.wait_send()

        @pl.when(owns(own_place))
        def _():
            spread_copy(turn, 1).wait_send()
            spread_copy(turn, 0).wait_send()

        return 0

    over_peers(drain, 0)

    @pl.when(owns(own_place))
    def _():
        spread_copy(22, 1).wait_send()

    for copy in sq_copies + core_copies + [y_copy, left_copy, right_copy] + w_copies + g_copies:
        copy.wait_send()
    for copy in waits:
        copy.wait_send()

    @pl.when(yl != yh)
    def _():
        for h in (0, 1):
            for n, (src, dst) in enumerate(pieces_of(h)):
                lend_copy(h, n, src, dst).wait_send()


def gather_and_power(gradient, basis, left_old):
    any_space = pl.BlockSpec(memory_space=pltpu.HBM)
    vmem = pl.BlockSpec(memory_space=pltpu.VMEM)
    dma = pltpu.SemaphoreType.DMA
    f32, bf16 = jnp.float32, jnp.bfloat16
    return pl.pallas_call(
        main_kernel,
        out_shape=(
            jax.ShapeDtypeStruct((4, 20, 16, 128), f32),
            jax.ShapeDtypeStruct((4, 80, 128), f32),
            jax.ShapeDtypeStruct((2, 80, 320), f32),
            jax.ShapeDtypeStruct((4, 8, 128), f32),
            jax.ShapeDtypeStruct((80, 640), f32),
            jax.ShapeDtypeStruct((80, 640), f32),
        ),
        in_specs=[any_space] * 3,
        out_specs=(vmem,) * 6,
        scratch_shapes=[
            pltpu.VMEM((2, 2, 4, 320, 384), bf16),
            pltpu.VMEM((2, 80, 640), bf16),
            pltpu.VMEM((4, 80, 384), f32),
            pltpu.VMEM((8, 128), f32),
            pltpu.VMEM((4, 80, 320), bf16),
            pltpu.VMEM((80, 640), f32),
            pltpu.VMEM((4, 80, 320), f32),
            pltpu.VMEM((4, 80, 320), f32),
            pltpu.VMEM((4, 80, 320), f32),
            pltpu.VMEM((2, 80, 128), f32),
            pltpu.VMEM((2, 80, 128), f32),
            pltpu.VMEM((20, 16, 128), f32),
            pltpu.VMEM((32, 16, 128), f32),
            dma((2, 3)), dma((2, 2, 16)), dma((64,)), dma((4,)), dma((1,)), dma((4,)), dma((2,)),
            dma((4,)), dma((4,)),
            dma((3,)), dma((4,)),
            dma((2,)), dma((4,)),
            dma((4,)), dma((4,)),
            dma((32,)), dma((32,)),
            dma((2, 32)), dma((2, 32)),
            dma((2,)), dma((4,)),
        ],
        compiler_params=pltpu.CompilerParams(
            collective_id=0, has_side_effects=True, vmem_limit_bytes=48 << 20
        ),
    )(*(pltpu.with_memory_space_constraint(v, pltpu.HBM) for v in (gradient, basis, left_old)))


def eliminate(block):
    n = 128
    sub = lax.broadcasted_iota(jnp.int32, (8, n), 0)
    lane = lax.broadcasted_iota(jnp.int32, (8, n), 1)
    m = [block[at : at + 8, :] for at in range(0, n, 8)]

    def columns_of(v, at):
        return [jnp.broadcast_to(v[:, at + j : at + j + 1], (8, n)) for j in range(8)]

    def row_of(v, j):
        return jnp.broadcast_to(v[j : j + 1, :], (8, n))

    cols = columns_of(m[0], 0)
    for b in range(n // 8):
        at = 8 * b
        inside = (lane >= at) & (lane < at + 8)
        rows = m[b]
        ahead = list(range(b + 1, min(b + 3, n // 8)))
        ahead_cols = {i: columns_of(m[i], at) for i in ahead}
        if ahead:
            later = columns_of(rows, at + 8)
            next_later = columns_of(m[b + 1], at + 8)
        ahead_rows = {i: jnp.where(inside, 0.0, m[i]) for i in ahead}
        rows = jnp.where(inside, (lane - at == sub).astype(jnp.float32), rows)
        for j in range(8):
            scale = lax.rsqrt(row_of(cols[j], j))
            below = jnp.where(sub > j, cols[j] * scale, 0.0)
            pivot = row_of(rows, j) * scale
            rows = jnp.where(sub == j, pivot, rows - below * pivot)
            ahead_below = {i: ahead_cols[i][j] * scale for i in ahead}
            for i in ahead:
                ahead_rows[i] = ahead_rows[i] - ahead_below[i] * pivot
            for k in range(j + 1, 8):
                row = row_of(cols[k], j) * scale
                cols[k] = cols[k] - below * row
                for i in ahead:
                    ahead_cols[i][k] = ahead_cols[i][k] - ahead_below[i] * row
            if ahead:
                for k in range(8):
                    row = row_of(later[k], j) * scale
                    later[k] = later[k] - below * row
                    next_later[k] = next_later[k] - ahead_below[b + 1] * row
        m[b] = rows
        for i in ahead:
            m[i] = ahead_rows[i]
        if ahead:
            cols = next_later
        if b + 3 < n // 8:
            change = full_dot(rows, rows, TN)
            for i in range(b + 3, n // 8):
                m[i] = jnp.where(inside, 0.0, m[i]) - change[8 * i : 8 * i + 8, :]
    return jnp.concatenate(m, axis=0)


def factor_kernel(
    gram_ref, w_ref, left_ref, sq_ref, ours_ref, theirs_ref, right_old_ref,
    left_stat_ref, right_stat_ref, q_ref, m_ref,
):
    order = 512
    n = 128
    role = 2 * lax.axis_index("yl") + lax.axis_index("core")
    weight = stat_weight(jnp.sum(sq_ref[0] + sq_ref[1] + sq_ref[2] + sq_ref[3]))[:1, :1]
    left_stat_ref[:, :320] = left_ref[0]
    left_stat_ref[:, 320:] = left_ref[1]
    right_stat_ref[...] = smoothing * right_old_ref[...] + weight * (ours_ref[...] + theirs_ref[...])
    for r in range(4):
        below, half_row = min(r + 1, 3), r % 2
        for t in range(8):
            at = n * r + 16 * t
            m_ref[at : at + 16, n * r : n * r + n] = gram_ref[r, t]
            at = n * below + 16 * t
            m_ref[at : at + 16, n * (r % 3) : n * (r % 3) + n] = gram_ref[r, 8 + t]
        for t in range(4):
            at = n * (2 + half_row) + 64 * (r // 2) + 16 * t
            m_ref[at : at + 16, n * half_row : n * half_row + n] = gram_ref[r, 16 + t]
        m_ref[order:, n * r : n * r + n] = w_ref[r]
    row = lax.broadcasted_iota(jnp.int32, (n, n), 0)
    col = lax.broadcasted_iota(jnp.int32, (n, n), 1)
    for at in range(0, order, n):
        end = at + n
        inverse = jnp.where(col <= row, eliminate(m_ref[at:end, at:end]), 0.0)
        panel = full_dot(m_ref[end:, at:end], inverse, NT)

        @pl.when(role == at // n)
        def _():
            q_ref[...] = panel[order - end :, :]

        for to in range(end, order, n):
            change = full_dot(panel[to - end :, :], panel[to - end : to - end + n, :], NT)
            m_ref[to:, to : to + n] = m_ref[to:, to : to + n] - change


def factor(gram, power, left, squares, ours, theirs, right_old):
    return pl.pallas_call(
        factor_kernel,
        out_shape=(
            jax.ShapeDtypeStruct((80, 640), jnp.float32),
            jax.ShapeDtypeStruct((80, 640), jnp.float32),
            jax.ShapeDtypeStruct((80, 128), jnp.float32),
        ),
        in_specs=[pl.BlockSpec(memory_space=pltpu.VMEM)] * 7,
        out_specs=(pl.BlockSpec(memory_space=pltpu.VMEM),) * 3,
        scratch_shapes=[pltpu.VMEM((592, 512), jnp.float32)],
        compiler_params=pltpu.CompilerParams(vmem_limit_bytes=32 << 20),
    )(gram, power, left, squares, ours, theirs, right_old)


def on_device(gradient, left_old, right_old, basis_old):
    gathered = gather_and_power(gradient, basis_old, left_old)
    return factor(*gathered, right_old)


def solution(mesh):
    finer = Mesh(mesh.devices.reshape(2, 2, 4, 2, 4), ("yl", "core", "z", "yh", "x"))
    return jax.shard_map(
        on_device,
        mesh=finer,
        in_specs=(P(SHARD, ROLE),) * 4,
        out_specs=(P(SHARD, ROLE),) * 3,
        check_vma=False,
    )
```

```python
import jax
import jax.numpy as jnp
from jax import lax
from jax.experimental import pallas as pl
from jax.experimental.pallas import tpu as pltpu
from jax.sharding import Mesh
from jax.sharding import PartitionSpec as P

SHARD = ("z", "yh", "x")
ROLE = ("yl", "core")
MESH = pl.DeviceIdType.MESH

smoothing = 0.95
clip_ratio = 4.0
epsilon_value = 1e-06

NN = (((1,), (0,)), ((), ()))
TN = (((0,), (0,)), ((), ()))
NT = (((1,), (1,)), ((), ()))


def bf16_dot(a, b, dims):
    return lax.dot_general(a, b, dims, preferred_element_type=jnp.float32)


def remote(src, dst, send_sem, recv_sem, **target):
    return pltpu.make_async_remote_copy(
        src_ref=src,
        dst_ref=dst,
        send_sem=send_sem,
        recv_sem=recv_sem,
        device_id=target,
        device_id_type=MESH,
    )


def arrived(ref, sem):
    pltpu.make_async_copy(ref, ref, sem).wait()


def ring(axis, step):
    return lax.rem(lax.axis_index(axis) + (4 + step), 4)


def greet(barrier, **target):
    pl.semaphore_signal(barrier, inc=1, device_id=target, device_id_type=MESH)


def stat_weight(squares):
    full = jnp.full((8, 128), squares + epsilon_value, jnp.float32)
    factor = jnp.minimum(1.0, clip_ratio * jnp.sqrt(jnp.float32(2560)) / jnp.sqrt(full))
    return (1.0 - smoothing) * (factor * factor)


def parts_of(x):
    high = x.astype(jnp.bfloat16)
    rest = x - high.astype(jnp.float32)
    middle = rest.astype(jnp.bfloat16)
    low = (rest - middle.astype(jnp.float32)).astype(jnp.bfloat16)
    return high, middle, low


def full_dot(a, b, dims):
    a_axis, b_axis = dims[0][0][0], dims[0][1][0]
    ah, am, al = parts_of(a)
    bh, bm, bl = (ah, am, al) if b is a else parts_of(b)
    left = jnp.concatenate([ah, ah, am, ah, al, am], axis=a_axis)
    right = jnp.concatenate([bh, bm, bh, bl, bh, bm], axis=b_axis)
    return bf16_dot(left, right, dims)


def main_kernel(
    gradient, basis, left_old,
    gram, power, left, squares, ours, theirs,
    blocks, mine, half, sq_sum, kept, right_out, partial, partial_in, stat, power_part, power_in, chunk, pieces,
    give, recv, send, send_y, recv_mine, recv_half, local_sem,
    send_core, recv_core, send_sq, recv_sq, send_w, recv_w, send_one, recv_one,
    send_rs, recv_rs, send_ag, recv_ag, send_g, recv_g,
):
    z, yh, x = (lax.axis_index(a) for a in SHARD)
    yl, core = (lax.axis_index(a) for a in ROLE)
    role = 2 * yl + core
    across = 2 * (1 - yl) + core
    shard = z * 8 + yh * 4 + x

    group = lax.rem(yl + yh, 2)
    strip_at = 2 * group + core
    strip_over = 2 * (1 - group) + core

    def peer(turn):
        at_z = lax.rem(z + 2 + turn // 8, 4)
        at_x = lax.rem(x + 2 + lax.rem(turn, 4), 4)
        at_yh = lax.rem(yh + 1 + lax.rem(turn // 4, 2), 2)
        at_yl = lax.rem(group + at_yh, 2)
        return at_z * 8 + at_yh * 4 + at_x, {"z": at_z, "yh": at_yh, "x": at_x, "yl": at_yl}

    def owner(place):
        return 5 * place["z"] + place["x"] + place["yh"]

    def owns(place):
        upper, low = place["yh"] == 1, place["x"] < 2
        return jnp.logical_or(
            jnp.logical_and(jnp.logical_not(upper), place["x"] < 3),
            jnp.logical_and(upper, jnp.logical_not(low)),
        )

    own_place = {"z": z, "yh": yh, "x": x}

    def over_peers(body, init):
        return lax.fori_loop(23, 32, body, lax.fori_loop(0, 22, body, init))

    barrier = pltpu.get_barrier_semaphore()
    for dh, dl, dc in ((0, 0, 1), (0, 1, 0), (0, 1, 1), (1, 0, 0), (1, 1, 0)):
        greet(
            barrier,
            yh=lax.rem(yh + dh, 2),
            yl=lax.rem(yl + dl, 2),
            core=lax.rem(core + dc, 2),
        )
    for axis in ("z", "x"):
        for step in (1, -1):
            greet(barrier, **{axis: ring(axis, step)})

    own_rows = pltpu.make_async_copy(gradient, mine.at[yl], local_sem.at[0])
    own_rows.start()
    own_half = pltpu.make_async_copy(
        left_old.at[:, pl.ds(pl.multiple_of(256 * yl, 128), 384)], half.at[role], local_sem.at[1]
    )
    own_half.start()
    sq_sum[...] = jnp.zeros((8, 128), jnp.float32)
    waits = []

    pl.semaphore_wait(barrier, 9)

    def unit(h, k, at_z, at_x):
        return blocks.at[h, k, at_z, pl.ds(pl.multiple_of(at_x * 80, 16), 80), :]

    def sem(h, k, at_z, at_x):
        return recv.at[h, k, at_z * 4 + at_x]

    def pieces_of(h):
        to = unit(h, yl, z, x)
        if h == 0:
            return [(gradient.at[:, :384], to)]
        return [(gradient.at[:, 384:], to.at[:, :256]), (basis, to.at[:, 256:])]

    def give_copy(h, n, src, dst):
        return remote(src, dst, give.at[0, h + n], sem(h, yl, z, x), yh=1 - yh, yl=yh)

    def lend_copy(h, n, src, dst):
        return remote(src, dst, give.at[1, h + n], sem(h, yl, z, x), yl=yh)

    for h in (0, 1):
        for n, (src, dst) in enumerate(pieces_of(h)):
            copy = give_copy(h, n, src, dst)
            waits.append(copy)

            @pl.when(yl != yh)
            def _():
                copy.start()

            @pl.when(yl == yh)
            def _():
                pltpu.make_async_copy(src, dst, sem(h, yl, z, x)).start()

            @pl.when(yl != yh)
            def _():
                lend_copy(h, n, src, dst).start()

    counter = [0]

    def push(h, k, at_z, at_x, axis, step):
        ref = unit(h, k, at_z, at_x)
        copy = remote(
            ref, ref, send.at[counter[0]], sem(h, k, at_z, at_x), **{axis: ring(axis, step)}
        )
        counter[0] += 1
        copy.start()
        waits.append(copy)

    def place(h, first, second):
        return (second, first) if h == 0 else (first, second)

    FIRST = ("x", "z")
    SECOND = ("z", "x")
    here = {"z": z, "x": x}

    def spread(h, k, onward, first, second):
        at_z, at_x = place(h, first, second)
        push(h, k, at_z, at_x, SECOND[h], onward)
        push(h, k, at_z, at_x, SECOND[h], -onward)

    def wait_unit(h, k, first, second):
        at_z, at_x = place(h, first, second)
        arrived(unit(h, k, at_z, at_x), sem(h, k, at_z, at_x))

    def add_squares(h, k, first, second):
        at_z, at_x = place(h, first, second)
        width = 384 if h == 0 else 256
        start = pl.multiple_of(at_x * 80, 16)
        value = blocks[h, k, at_z, pl.ds(start, 80), :width].astype(jnp.float32)
        value = value * value
        wide = value[:, :128]
        for lane in range(128, width, 128):
            wide = wide + value[:, lane : lane + 128]
        total = wide[:8]
        for row in range(8, 80, 8):
            total = total + wide[row : row + 8]
        sq_sum[...] += total

    def step_one(h, k, first, second, step):
        at_z, at_x = place(h, first, second)
        push(h, k, at_z, at_x, FIRST[h], step)

    both = [(k, h, onward) for k, onward in ((yh, 1), (1 - yh, -1)) for h in (0, 1)]

    for turn, (k, h, onward) in enumerate(both):
        wait_unit(h, k, here[FIRST[h]], here[SECOND[h]])
        step_one(h, k, here[FIRST[h]], here[SECOND[h]], onward)
        step_one(h, k, here[FIRST[h]], here[SECOND[h]], -onward)
        if turn == 2:
            @pl.when(yl == yh)
            def _():
                for half_at in (0, 1):
                    for n, (src, dst) in enumerate(pieces_of(half_at)):
                        give_copy(half_at, n, src, dst).start()
    for toward in (1, -1):
        for k, h, onward in both:
            at_z, at_x = place(h, here[FIRST[h]], here[SECOND[h]])
            push(h, k, at_z, at_x, SECOND[h], toward * onward)
    to_partner = remote(gradient, mine.at[yl], send_y.at[0], recv_mine.at[0], yl=1 - yl)
    to_partner.start()
    waits.append(to_partner)
    to_core = remote(
        left_old.at[:, pl.ds(pl.multiple_of(256 * yl, 128), 384)],
        half.at[role],
        send_y.at[1],
        recv_half.at[role],
        core=1 - core,
    )
    to_core.start()
    waits.append(to_core)
    for k, h, onward in both:
        add_squares(h, k, here[FIRST[h]], here[SECOND[h]])
    for k, h, onward in both:
        behind = ring(FIRST[h], -onward)
        wait_unit(h, k, behind, here[SECOND[h]])
        step_one(h, k, behind, here[SECOND[h]], onward)
    for k, h, onward in both:
        spread(h, k, onward, ring(FIRST[h], -onward), here[SECOND[h]])
    for k, h, onward in both:
        ahead = ring(FIRST[h], onward)
        wait_unit(h, k, ahead, here[SECOND[h]])
        spread(h, k, onward, ahead, here[SECOND[h]])
    for k, h, onward in both:
        add_squares(h, k, ring(FIRST[h], -onward), here[SECOND[h]])
        add_squares(h, k, ring(FIRST[h], onward), here[SECOND[h]])
    for k, h, onward in both:
        far = ring(FIRST[h], 2)
        wait_unit(h, k, far, here[SECOND[h]])
        spread(h, k, onward, far, here[SECOND[h]])

    for dc in (0, 1):
        over = remote(
            left_old.at[:, pl.ds(pl.multiple_of(256 * (1 - yl), 128), 384)],
            half.at[role],
            send_y.at[2 + dc],
            recv_half.at[role],
            yl=1 - yl,
            core=lax.rem(core + dc, 2),
        )
        over.start()
        waits.append(over)
    for k, h, onward in both:
        add_squares(h, k, ring(FIRST[h], 2), here[SECOND[h]])

    def column(h, onward, turn):
        return ring(FIRST[h], (0, -onward, onward, 2)[turn])

    for turn in range(4):
        for k, h, onward in both:
            behind = ring(SECOND[h], -onward)
            first = column(h, onward, turn)
            wait_unit(h, k, first, behind)
            at_z, at_x = place(h, first, behind)
            push(h, k, at_z, at_x, SECOND[h], onward)
        for k, h, onward in both:
            add_squares(h, k, column(h, onward, turn), ring(SECOND[h], -onward))
    own_half.wait()
    for dl, dc in ((0, 1), (1, 0), (1, 1)):
        other = 2 * lax.rem(yl + dl, 2) + lax.rem(core + dc, 2)
        arrived(half.at[other], recv_half.at[other])
    for at_z in range(4):
        held = half[at_z]
        stat[at_z] = smoothing * jnp.where(yl == 0, held[:, :320], held[:, 64:])
    for turn in range(4):
        for k, h, onward in both:
            first = column(h, onward, turn)
            ahead, far = ring(SECOND[h], onward), ring(SECOND[h], 2)
            wait_unit(h, k, first, ahead)
            add_squares(h, k, first, ahead)
            wait_unit(h, k, first, far)
            add_squares(h, k, first, far)
    own_rows.wait()
    arrived(mine.at[1 - yl], recv_mine.at[0])

    squares[role] = sq_sum[...]
    sq_copies = []
    for n, (dl, dc) in enumerate(((1, 0), (0, 1), (1, 1))):
        copy = remote(
            squares.at[role],
            squares.at[role],
            send_sq.at[n],
            recv_sq.at[role],
            yl=lax.rem(yl + dl, 2),
            core=lax.rem(core + dc, 2),
        )
        copy.start()
        sq_copies.append(copy)
    core_copies = []
    for at_z in range(4):
        total = jnp.zeros((80, 320), jnp.float32)
        for k in (0, 1):
            total += bf16_dot(mine[k, :, :384], blocks[0, k, at_z], NT)
            total += bf16_dot(mine[k, :, 384:], blocks[1, k, at_z, :, :256], NT)
        partial[at_z] = total
        copy = remote(
            partial.at[at_z],
            partial_in.at[at_z],
            send_core.at[at_z],
            recv_core.at[at_z],
            core=1 - core,
        )
        copy.start()
        core_copies.append(copy)

    for dl, dc in ((0, 1), (1, 0), (1, 1)):
        other = 2 * lax.rem(yl + dl, 2) + lax.rem(core + dc, 2)
        arrived(squares.at[other], recv_sq.at[other])
    all_squares = jnp.sum(squares[0] + squares[1] + squares[2] + squares[3])
    weight = stat_weight(all_squares)[:1, :1]

    stacked = []
    for at_z in range(4):
        core_copies[at_z].wait_recv()
        value = stat[at_z] + weight * (partial[at_z] + partial_in[at_z])
        stat[at_z] = value
        stacked.append(jnp.concatenate(parts_of(value), axis=0))
    y_copies = []
    for k in (0, 1):
        total = jnp.zeros((80, 128), jnp.float32)
        for at_z in range(4):
            product = bf16_dot(stacked[at_z], blocks[1, k, at_z, :, 256:], NN)
            total = total + (product[:80] + product[80:160] + product[160:])
        power_part[k] = total
        copy = remote(
            power_part.at[k], power_in.at[k], send_one.at[4 * k], recv_one.at[4 * k], yl=1 - yl
        )
        copy.start()
        y_copies.append(copy)
    left[yl] = stat[role]
    left_copy = remote(stat.at[across], left.at[yl], send_one.at[1], recv_one.at[1], yl=1 - yl)
    left_copy.start()

    has_columns = core == lax.rem(z, 2)
    kept_copy = remote(kept, kept, send_one.at[2], recv_one.at[2], core=1 - core)

    @pl.when(has_columns)
    def _():
        offset = 80 * (4 * yh + x)
        row = lax.broadcasted_iota(jnp.int32, (80, 640), 0)
        col = lax.broadcasted_iota(jnp.int32, (80, 640), 1)
        pick = jnp.where(col == row + offset, 1.0, 0.0).astype(jnp.bfloat16)
        for at_z in range(4):
            chosen = bf16_dot(pick[:, :384], blocks[0, z // 2, at_z], NT)
            chosen += bf16_dot(pick[:, 384:], blocks[1, z // 2, at_z, :, :256], NT)
            kept[at_z] = chosen.astype(jnp.bfloat16)
        kept_copy.start()

    w_copies = []
    for k in (0, 1):
        y_copies[k].wait_recv()
        slot = 2 * k + core
        power[slot] = power_part[k] + power_in[k]
        copy = remote(power.at[slot], power.at[slot], send_w.at[k], recv_w.at[slot], core=1 - core)
        copy.start()
        w_copies.append(copy)
    for k in (0, 1):
        slot = 2 * k + 1 - core
        arrived(power.at[slot], recv_w.at[slot])

    def block(a, b):
        return full_dot(power[a], power[b], TN)

    half_row = lax.rem(strip_at, 2)
    thirds = (
        block(strip_at, strip_at),
        block(jnp.minimum(strip_at + 1, 3), lax.rem(strip_at, 3)),
        block(2 + half_row, half_row),
    )
    for n in (0, 1):
        for t in range(8):
            chunk[8 * n + t] = thirds[n][16 * t : 16 * t + 16]
    lower_half = jnp.where(strip_at < 2, thirds[2][:64], thirds[2][64:])
    for t in range(4):
        chunk[16 + t] = lower_half[16 * t : 16 * t + 16]

    def scatter_copy(turn):
        other, place = peer(turn)
        copy = remote(
            chunk.at[owner(place)],
            pieces.at[shard],
            send_rs.at[other],
            recv_rs.at[shard],
            **place,
        )
        return place, copy

    def scatter_start(turn, _):
        place, copy = scatter_copy(turn)

        @pl.when(owns(place))
        def _():
            copy.start()

        return 0

    over_peers(scatter_start, 0)

    @pl.when(jnp.logical_not(has_columns))
    def _():
        arrived(kept, recv_one.at[2])

    def right_product(k, out):
        for h, width in ((0, 384), (1, 256)):
            total = jnp.zeros((80, width), jnp.float32)
            for at_z in range(4):
                total += bf16_dot(kept[at_z], blocks[h, k, at_z, :, :width], NN)
            out[:, 384 * h : 384 * h + width] = total

    right_product(1 - yl, right_out)
    right_copy = remote(right_out, theirs, send_one.at[3], recv_one.at[3], yl=1 - yl)
    right_copy.start()

    def scatter_arrive(turn, total):
        other, _ = peer(turn)
        arrived(pieces.at[other], recv_rs.at[other])
        return total + pieces[other]

    def spread_copy(turn, flip):
        other, place = peer(turn)
        if flip:
            place = dict(place, yl=1 - place["yl"])
        pair = gram.at[strip_at, owner(own_place)]
        return remote(pair, pair, send_ag.at[flip, other], recv_ag.at[flip, shard], **place)

    def spread_start(turn, _):
        spread_copy(turn, 1).start()
        spread_copy(turn, 0).start()
        return 0

    @pl.when(owns(own_place))
    def _():
        gram[strip_at, owner(own_place)] = over_peers(scatter_arrive, chunk[owner(own_place)])
        over_peers(spread_start, 0)
        spread_copy(22, 1).start()

    right_product(yl, ours)

    def pair_arrives(flip, other, place):
        strip = strip_over if flip else strip_at

        @pl.when(owns(place))
        def _():
            arrived(gram.at[strip, owner(place)], recv_ag.at[flip, other])

    g_copies = []
    for flip, strip in ((1, strip_over), (0, strip_at)):

        def spread_arrive(turn, _):
            other, place = peer(turn)
            pair_arrives(flip, other, place)
            return 0

        if flip:
            pair_arrives(1, shard, own_place)
        over_peers(spread_arrive, 0)
        copy = remote(
            gram.at[strip], gram.at[strip], send_g.at[flip], recv_g.at[strip], core=1 - core
        )
        copy.start()
        g_copies.append(copy)
    for k in (0, 1):
        slot = 2 * k + 1 - core
        arrived(gram.at[slot], recv_g.at[slot])

    arrived(left.at[1 - yl], recv_one.at[1])
    arrived(theirs, recv_one.at[3])

    @pl.when(has_columns)
    def _():
        kept_copy.wait_send()

    def drain(turn, _):
        place, copy = scatter_copy(turn)

        @pl.when(owns(place))
        def _():
            copy.wait_send()

        @pl.when(owns(own_place))
        def _():
            spread_copy(turn, 1).wait_send()
            spread_copy(turn, 0).wait_send()

        return 0

    over_peers(drain, 0)

    @pl.when(owns(own_place))
    def _():
        spread_copy(22, 1).wait_send()

    for copy in sq_copies + core_copies + y_copies + [left_copy, right_copy] + w_copies + g_copies:
        copy.wait_send()
    for copy in waits:
        copy.wait_send()

    @pl.when(yl != yh)
    def _():
        for h in (0, 1):
            for n, (src, dst) in enumerate(pieces_of(h)):
                lend_copy(h, n, src, dst).wait_send()


def gather_and_power(gradient, basis, left_old):
    any_space = pl.BlockSpec(memory_space=pltpu.HBM)
    vmem = pl.BlockSpec(memory_space=pltpu.VMEM)
    dma = pltpu.SemaphoreType.DMA
    f32, bf16 = jnp.float32, jnp.bfloat16
    return pl.pallas_call(
        main_kernel,
        out_shape=(
            jax.ShapeDtypeStruct((4, 20, 16, 128), f32),
            jax.ShapeDtypeStruct((4, 80, 128), f32),
            jax.ShapeDtypeStruct((2, 80, 320), f32),
            jax.ShapeDtypeStruct((4, 8, 128), f32),
            jax.ShapeDtypeStruct((80, 640), f32),
            jax.ShapeDtypeStruct((80, 640), f32),
        ),
        in_specs=[any_space] * 3,
        out_specs=(vmem,) * 6,
        scratch_shapes=[
            pltpu.VMEM((2, 2, 4, 320, 384), bf16),
            pltpu.VMEM((2, 80, 640), bf16),
            pltpu.VMEM((4, 80, 384), f32),
            pltpu.VMEM((8, 128), f32),
            pltpu.VMEM((4, 80, 320), bf16),
            pltpu.VMEM((80, 640), f32),
            pltpu.VMEM((4, 80, 320), f32),
            pltpu.VMEM((4, 80, 320), f32),
            pltpu.VMEM((4, 80, 320), f32),
            pltpu.VMEM((2, 80, 128), f32),
            pltpu.VMEM((2, 80, 128), f32),
            pltpu.VMEM((20, 16, 128), f32),
            pltpu.VMEM((32, 16, 128), f32),
            dma((2, 3)), dma((2, 2, 16)), dma((64,)), dma((4,)), dma((1,)), dma((4,)), dma((2,)),
            dma((4,)), dma((4,)),
            dma((3,)), dma((4,)),
            dma((2,)), dma((4,)),
            dma((5,)), dma((5,)),
            dma((32,)), dma((32,)),
            dma((2, 32)), dma((2, 32)),
            dma((2,)), dma((4,)),
        ],
        compiler_params=pltpu.CompilerParams(
            collective_id=0, has_side_effects=True, vmem_limit_bytes=48 << 20
        ),
    )(*(pltpu.with_memory_space_constraint(v, pltpu.HBM) for v in (gradient, basis, left_old)))


def eliminate(block):
    n = 128
    sub = lax.broadcasted_iota(jnp.int32, (8, n), 0)
    lane = lax.broadcasted_iota(jnp.int32, (8, n), 1)
    m = [block[at : at + 8, :] for at in range(0, n, 8)]

    def columns_of(v, at):
        return [jnp.broadcast_to(v[:, at + j : at + j + 1], (8, n)) for j in range(8)]

    def row_of(v, j):
        return jnp.broadcast_to(v[j : j + 1, :], (8, n))

    cols = columns_of(m[0], 0)
    for b in range(n // 8):
        at = 8 * b
        inside = (lane >= at) & (lane < at + 8)
        rows = m[b]
        ahead = list(range(b + 1, min(b + 3, n // 8)))
        ahead_cols = {i: columns_of(m[i], at) for i in ahead}
        if ahead:
            later = columns_of(rows, at + 8)
            next_later = columns_of(m[b + 1], at + 8)
        ahead_rows = {i: jnp.where(inside, 0.0, m[i]) for i in ahead}
        rows = jnp.where(inside, (lane - at == sub).astype(jnp.float32), rows)
        for j in range(8):
            scale = lax.rsqrt(row_of(cols[j], j))
            below = jnp.where(sub > j, cols[j] * scale, 0.0)
            pivot = row_of(rows, j) * scale
            rows = jnp.where(sub == j, pivot, rows - below * pivot)
            ahead_below = {i: ahead_cols[i][j] * scale for i in ahead}
            for i in ahead:
                ahead_rows[i] = ahead_rows[i] - ahead_below[i] * pivot
            for k in range(j + 1, 8):
                row = row_of(cols[k], j) * scale
                cols[k] = cols[k] - below * row
                for i in ahead:
                    ahead_cols[i][k] = ahead_cols[i][k] - ahead_below[i] * row
            if ahead:
                for k in range(8):
                    row = row_of(later[k], j) * scale
                    later[k] = later[k] - below * row
                    next_later[k] = next_later[k] - ahead_below[b + 1] * row
        m[b] = rows
        for i in ahead:
            m[i] = ahead_rows[i]
        if ahead:
            cols = next_later
        if b + 3 < n // 8:
            change = full_dot(rows, rows, TN)
            for i in range(b + 3, n // 8):
                m[i] = jnp.where(inside, 0.0, m[i]) - change[8 * i : 8 * i + 8, :]
    return jnp.concatenate(m, axis=0)


def factor_kernel(
    gram_ref, w_ref, left_ref, sq_ref, ours_ref, theirs_ref, right_old_ref,
    left_stat_ref, right_stat_ref, q_ref, m_ref,
):
    order = 512
    n = 128
    role = 2 * lax.axis_index("yl") + lax.axis_index("core")
    weight = stat_weight(jnp.sum(sq_ref[0] + sq_ref[1] + sq_ref[2] + sq_ref[3]))[:1, :1]
    left_stat_ref[:, :320] = left_ref[0]
    left_stat_ref[:, 320:] = left_ref[1]
    right_stat_ref[...] = smoothing * right_old_ref[...] + weight * (ours_ref[...] + theirs_ref[...])
    for r in range(4):
        below, half_row = min(r + 1, 3), r % 2
        for t in range(8):
            at = n * r + 16 * t
            m_ref[at : at + 16, n * r : n * r + n] = gram_ref[r, t]
            at = n * below + 16 * t
            m_ref[at : at + 16, n * (r % 3) : n * (r % 3) + n] = gram_ref[r, 8 + t]
        for t in range(4):
            at = n * (2 + half_row) + 64 * (r // 2) + 16 * t
            m_ref[at : at + 16, n * half_row : n * half_row + n] = gram_ref[r, 16 + t]
        m_ref[order:, n * r : n * r + n] = w_ref[r]
    row = lax.broadcasted_iota(jnp.int32, (n, n), 0)
    col = lax.broadcasted_iota(jnp.int32, (n, n), 1)
    for at in range(0, order, n):
        end = at + n
        inverse = jnp.where(col <= row, eliminate(m_ref[at:end, at:end]), 0.0)
        panel = full_dot(m_ref[end:, at:end], inverse, NT)

        @pl.when(role == at // n)
        def _():
            q_ref[...] = panel[order - end :, :]

        for to in range(end, order, n):
            change = full_dot(panel[to - end :, :], panel[to - end : to - end + n, :], NT)
            m_ref[to:, to : to + n] = m_ref[to:, to : to + n] - change


def factor(gram, power, left, squares, ours, theirs, right_old):
    return pl.pallas_call(
        factor_kernel,
        out_shape=(
            jax.ShapeDtypeStruct((80, 640), jnp.float32),
            jax.ShapeDtypeStruct((80, 640), jnp.float32),
            jax.ShapeDtypeStruct((80, 128), jnp.float32),
        ),
        in_specs=[pl.BlockSpec(memory_space=pltpu.VMEM)] * 7,
        out_specs=(pl.BlockSpec(memory_space=pltpu.VMEM),) * 3,
        scratch_shapes=[pltpu.VMEM((592, 512), jnp.float32)],
        compiler_params=pltpu.CompilerParams(vmem_limit_bytes=32 << 20),
    )(gram, power, left, squares, ours, theirs, right_old)


def on_device(gradient, left_old, right_old, basis_old):
    gathered = gather_and_power(gradient, basis_old, left_old)
    return factor(*gathered, right_old)


def solution(mesh):
    finer = Mesh(mesh.devices.reshape(2, 2, 4, 2, 4), ("yl", "core", "z", "yh", "x"))
    return jax.shard_map(
        on_device,
        mesh=finer,
        in_specs=(P(SHARD, ROLE),) * 4,
        out_specs=(P(SHARD, ROLE),) * 3,
        check_vma=False,
    )
```

```python
import jax
import jax.numpy as jnp
from jax import lax
from jax.experimental import pallas as pl
from jax.experimental.pallas import tpu as pltpu
from jax.sharding import Mesh
from jax.sharding import PartitionSpec as P

SHARD = ("z", "yh", "x")
ROLE = ("yl", "core")
MESH = pl.DeviceIdType.MESH

smoothing = 0.95
clip_ratio = 4.0
epsilon_value = 1e-06

NN = (((1,), (0,)), ((), ()))
TN = (((0,), (0,)), ((), ()))
NT = (((1,), (1,)), ((), ()))


def bf16_dot(a, b, dims):
    return lax.dot_general(a, b, dims, preferred_element_type=jnp.float32)


def remote(src, dst, send_sem, recv_sem, **target):
    return pltpu.make_async_remote_copy(
        src_ref=src,
        dst_ref=dst,
        send_sem=send_sem,
        recv_sem=recv_sem,
        device_id=target,
        device_id_type=MESH,
    )


def arrived(ref, sem):
    pltpu.make_async_copy(ref, ref, sem).wait()


def ring(axis, step):
    return lax.rem(lax.axis_index(axis) + (4 + step), 4)


def greet(barrier, **target):
    pl.semaphore_signal(barrier, inc=1, device_id=target, device_id_type=MESH)


def stat_weight(squares):
    full = jnp.full((8, 128), squares + epsilon_value, jnp.float32)
    factor = jnp.minimum(1.0, clip_ratio * jnp.sqrt(jnp.float32(2560)) / jnp.sqrt(full))
    return (1.0 - smoothing) * (factor * factor)


def parts_of(x):
    high = x.astype(jnp.bfloat16)
    rest = x - high.astype(jnp.float32)
    middle = rest.astype(jnp.bfloat16)
    low = (rest - middle.astype(jnp.float32)).astype(jnp.bfloat16)
    return high, middle, low


def full_dot(a, b, dims):
    a_axis, b_axis = dims[0][0][0], dims[0][1][0]
    ah, am, al = parts_of(a)
    bh, bm, bl = (ah, am, al) if b is a else parts_of(b)
    left = jnp.concatenate([ah, ah, am, ah, al, am], axis=a_axis)
    right = jnp.concatenate([bh, bm, bh, bl, bh, bm], axis=b_axis)
    return bf16_dot(left, right, dims)


def main_kernel(
    gradient, basis, left_old,
    gram, power, left, squares, ours, theirs,
    blocks, mine, half, sq_sum, kept, right_out, partial, partial_in, stat, power_part, power_in, chunk, pieces,
    give, recv, send, send_y, recv_mine, recv_half, local_sem,
    send_core, recv_core, send_sq, recv_sq, send_w, recv_w, send_one, recv_one,
    send_rs, recv_rs, send_ag, recv_ag, send_g, recv_g,
):
    z, yh, x = (lax.axis_index(a) for a in SHARD)
    yl, core = (lax.axis_index(a) for a in ROLE)
    role = 2 * yl + core
    across = 2 * (1 - yl) + core
    shard = z * 8 + yh * 4 + x

    group = lax.rem(yl + yh, 2)
    strip_at = 2 * group + core
    strip_over = 2 * (1 - group) + core

    def peer(turn):
        at_z = lax.rem(z + 2 + turn // 8, 4)
        at_x = lax.rem(x + 2 + lax.rem(turn, 4), 4)
        at_yh = lax.rem(yh + 1 + lax.rem(turn // 4, 2), 2)
        at_yl = lax.rem(group + at_yh, 2)
        return at_z * 8 + at_yh * 4 + at_x, {"z": at_z, "yh": at_yh, "x": at_x, "yl": at_yl}

    def owner(place):
        return 5 * place["z"] + place["x"] + place["yh"]

    def owns(place):
        upper, low = place["yh"] == 1, place["x"] < 2
        return jnp.logical_or(
            jnp.logical_and(jnp.logical_not(upper), place["x"] < 3),
            jnp.logical_and(upper, jnp.logical_not(low)),
        )

    own_place = {"z": z, "yh": yh, "x": x}

    def over_peers(body, init):
        return lax.fori_loop(23, 32, body, lax.fori_loop(0, 22, body, init))

    barrier = pltpu.get_barrier_semaphore()
    for dh, dl, dc in ((0, 0, 1), (0, 1, 0), (0, 1, 1), (1, 0, 0), (1, 1, 0)):
        greet(
            barrier,
            yh=lax.rem(yh + dh, 2),
            yl=lax.rem(yl + dl, 2),
            core=lax.rem(core + dc, 2),
        )
    for axis in ("z", "x"):
        for step in (1, -1):
            greet(barrier, **{axis: ring(axis, step)})

    own_rows = pltpu.make_async_copy(gradient, mine.at[yl], local_sem.at[0])
    own_rows.start()
    own_half = pltpu.make_async_copy(
        left_old.at[:, pl.ds(pl.multiple_of(256 * yl, 128), 384)], half.at[role], local_sem.at[1]
    )
    own_half.start()
    sq_sum[...] = jnp.zeros((8, 128), jnp.float32)
    waits = []

    pl.semaphore_wait(barrier, 9)

    def unit(h, k, at_z, at_x):
        return blocks.at[h, k, at_z, pl.ds(pl.multiple_of(at_x * 80, 16), 80), :]

    def sem(h, k, at_z, at_x):
        return recv.at[h, k, at_z * 4 + at_x]

    def pieces_of(h):
        to = unit(h, yl, z, x)
        if h == 0:
            return [(gradient.at[:, :384], to)]
        return [(gradient.at[:, 384:], to.at[:, :256]), (basis, to.at[:, 256:])]

    def give_copy(h, n, src, dst):
        return remote(src, dst, give.at[0, h + n], sem(h, yl, z, x), yh=1 - yh, yl=yh)

    def lend_copy(h, n, src, dst):
        return remote(src, dst, give.at[1, h + n], sem(h, yl, z, x), yl=yh)

    for h in (0, 1):
        for n, (src, dst) in enumerate(pieces_of(h)):
            copy = give_copy(h, n, src, dst)
            waits.append(copy)

            @pl.when(yl != yh)
            def _():
                copy.start()

            @pl.when(yl == yh)
            def _():
                pltpu.make_async_copy(src, dst, sem(h, yl, z, x)).start()

            @pl.when(yl != yh)
            def _():
                lend_copy(h, n, src, dst).start()

    counter = [0]

    def push(h, k, at_z, at_x, axis, step):
        ref = unit(h, k, at_z, at_x)
        copy = remote(
            ref, ref, send.at[counter[0]], sem(h, k, at_z, at_x), **{axis: ring(axis, step)}
        )
        counter[0] += 1
        copy.start()
        waits.append(copy)

    def place(h, first, second):
        return (second, first) if h == 0 else (first, second)

    FIRST = ("x", "z")
    SECOND = ("z", "x")
    here = {"z": z, "x": x}

    def spread(h, k, onward, first, second):
        at_z, at_x = place(h, first, second)
        push(h, k, at_z, at_x, SECOND[h], onward)
        push(h, k, at_z, at_x, SECOND[h], -onward)

    def wait_unit(h, k, first, second):
        at_z, at_x = place(h, first, second)
        arrived(unit(h, k, at_z, at_x), sem(h, k, at_z, at_x))

    def add_squares(h, k, first, second):
        at_z, at_x = place(h, first, second)
        width = 384 if h == 0 else 256
        start = pl.multiple_of(at_x * 80, 16)
        value = blocks[h, k, at_z, pl.ds(start, 80), :width].astype(jnp.float32)
        value = value * value
        wide = value[:, :128]
        for lane in range(128, width, 128):
            wide = wide + value[:, lane : lane + 128]
        total = wide[:8]
        for row in range(8, 80, 8):
            total = total + wide[row : row + 8]
        sq_sum[...] += total

    def step_one(h, k, first, second, step):
        at_z, at_x = place(h, first, second)
        push(h, k, at_z, at_x, FIRST[h], step)

    both = [(k, h, onward) for k, onward in ((yh, 1), (1 - yh, -1)) for h in (0, 1)]

    for turn, (k, h, onward) in enumerate(both):
        wait_unit(h, k, here[FIRST[h]], here[SECOND[h]])
        step_one(h, k, here[FIRST[h]], here[SECOND[h]], onward)
        step_one(h, k, here[FIRST[h]], here[SECOND[h]], -onward)
        if turn == 2:
            @pl.when(yl == yh)
            def _():
                for half_at in (0, 1):
                    for n, (src, dst) in enumerate(pieces_of(half_at)):
                        give_copy(half_at, n, src, dst).start()
    for toward in (1, -1):
        for k, h, onward in both:
            at_z, at_x = place(h, here[FIRST[h]], here[SECOND[h]])
            push(h, k, at_z, at_x, SECOND[h], toward * onward)
    to_partner = remote(gradient, mine.at[yl], send_y.at[0], recv_mine.at[0], yl=1 - yl)
    to_partner.start()
    waits.append(to_partner)
    to_core = remote(
        left_old.at[:, pl.ds(pl.multiple_of(256 * yl, 128), 384)],
        half.at[role],
        send_y.at[1],
        recv_half.at[role],
        core=1 - core,
    )
    to_core.start()
    waits.append(to_core)
    for k, h, onward in both:
        add_squares(h, k, here[FIRST[h]], here[SECOND[h]])
    for k, h, onward in both:
        behind = ring(FIRST[h], -onward)
        wait_unit(h, k, behind, here[SECOND[h]])
        step_one(h, k, behind, here[SECOND[h]], onward)
    for k, h, onward in both:
        spread(h, k, onward, ring(FIRST[h], -onward), here[SECOND[h]])
    for k, h, onward in both:
        ahead = ring(FIRST[h], onward)
        wait_unit(h, k, ahead, here[SECOND[h]])
        spread(h, k, onward, ahead, here[SECOND[h]])
    for k, h, onward in both:
        add_squares(h, k, ring(FIRST[h], -onward), here[SECOND[h]])
        add_squares(h, k, ring(FIRST[h], onward), here[SECOND[h]])
    for k, h, onward in both:
        far = ring(FIRST[h], 2)
        wait_unit(h, k, far, here[SECOND[h]])
        spread(h, k, onward, far, here[SECOND[h]])

    for dc in (0, 1):
        over = remote(
            left_old.at[:, pl.ds(pl.multiple_of(256 * (1 - yl), 128), 384)],
            half.at[role],
            send_y.at[2 + dc],
            recv_half.at[role],
            yl=1 - yl,
            core=lax.rem(core + dc, 2),
        )
        over.start()
        waits.append(over)
    for k, h, onward in both:
        add_squares(h, k, ring(FIRST[h], 2), here[SECOND[h]])

    def column(h, onward, turn):
        return ring(FIRST[h], (0, -onward, onward, 2)[turn])

    for turn in range(4):
        for k, h, onward in both:
            behind = ring(SECOND[h], -onward)
            first = column(h, onward, turn)
            wait_unit(h, k, first, behind)
            at_z, at_x = place(h, first, behind)
            push(h, k, at_z, at_x, SECOND[h], onward)
        for k, h, onward in both:
            add_squares(h, k, column(h, onward, turn), ring(SECOND[h], -onward))
    own_half.wait()
    for dl, dc in ((0, 1), (1, 0), (1, 1)):
        other = 2 * lax.rem(yl + dl, 2) + lax.rem(core + dc, 2)
        arrived(half.at[other], recv_half.at[other])
    for at_z in range(4):
        held = half[at_z]
        stat[at_z] = smoothing * jnp.where(yl == 0, held[:, :320], held[:, 64:])
    for turn in range(4):
        for k, h, onward in both:
            first = column(h, onward, turn)
            ahead, far = ring(SECOND[h], onward), ring(SECOND[h], 2)
            wait_unit(h, k, first, ahead)
            add_squares(h, k, first, ahead)
            wait_unit(h, k, first, far)
            add_squares(h, k, first, far)
    own_rows.wait()
    arrived(mine.at[1 - yl], recv_mine.at[0])

    squares[role] = sq_sum[...]
    sq_copies = []
    for n, (dl, dc) in enumerate(((1, 0), (0, 1), (1, 1))):
        copy = remote(
            squares.at[role],
            squares.at[role],
            send_sq.at[n],
            recv_sq.at[role],
            yl=lax.rem(yl + dl, 2),
            core=lax.rem(core + dc, 2),
        )
        copy.start()
        sq_copies.append(copy)
    core_copies = []
    for at_z in range(4):
        total = jnp.zeros((80, 320), jnp.float32)
        for k in (0, 1):
            total += bf16_dot(mine[k, :, :384], blocks[0, k, at_z], NT)
            total += bf16_dot(mine[k, :, 384:], blocks[1, k, at_z, :, :256], NT)
        partial[at_z] = total
        copy = remote(
            partial.at[at_z],
            partial_in.at[at_z],
            send_core.at[at_z],
            recv_core.at[at_z],
            core=1 - core,
        )
        copy.start()
        core_copies.append(copy)

    for dl, dc in ((0, 1), (1, 0), (1, 1)):
        other = 2 * lax.rem(yl + dl, 2) + lax.rem(core + dc, 2)
        arrived(squares.at[other], recv_sq.at[other])
    all_squares = jnp.sum(squares[0] + squares[1] + squares[2] + squares[3])
    weight = stat_weight(all_squares)[:1, :1]

    stacked = []
    for at_z in range(4):
        core_copies[at_z].wait_recv()
        value = stat[at_z] + weight * (partial[at_z] + partial_in[at_z])
        stat[at_z] = value
        stacked.append(jnp.concatenate(parts_of(value), axis=0))
    y_copies = []
    for k in (0, 1):
        total = jnp.zeros((80, 128), jnp.float32)
        for at_z in range(4):
            product = bf16_dot(stacked[at_z], blocks[1, k, at_z, :, 256:], NN)
            total = total + (product[:80] + product[80:160] + product[160:])
        power_part[k] = total
        copy = remote(
            power_part.at[k], power_in.at[k], send_one.at[4 * k], recv_one.at[4 * k], yl=1 - yl
        )
        copy.start()
        y_copies.append(copy)
    left[yl] = stat[role]
    left_copy = remote(stat.at[across], left.at[yl], send_one.at[1], recv_one.at[1], yl=1 - yl)
    left_copy.start()

    has_columns = core == lax.rem(z, 2)
    kept_copy = remote(kept, kept, send_one.at[2], recv_one.at[2], core=1 - core)

    @pl.when(has_columns)
    def _():
        offset = 80 * (4 * yh + x)
        row = lax.broadcasted_iota(jnp.int32, (80, 640), 0)
        col = lax.broadcasted_iota(jnp.int32, (80, 640), 1)
        pick = jnp.where(col == row + offset, 1.0, 0.0).astype(jnp.bfloat16)
        for at_z in range(4):
            chosen = bf16_dot(pick[:, :384], blocks[0, z // 2, at_z], NT)
            chosen += bf16_dot(pick[:, 384:], blocks[1, z // 2, at_z, :, :256], NT)
            kept[at_z] = chosen.astype(jnp.bfloat16)
        kept_copy.start()

    w_copies = []
    for k in (0, 1):
        y_copies[k].wait_recv()
        slot = 2 * k + core
        power[slot] = power_part[k] + power_in[k]
        copy = remote(power.at[slot], power.at[slot], send_w.at[k], recv_w.at[slot], core=1 - core)
        copy.start()
        w_copies.append(copy)
    for k in (0, 1):
        slot = 2 * k + 1 - core
        arrived(power.at[slot], recv_w.at[slot])

    def block(a, b):
        return full_dot(power[a], power[b], TN)

    half_row = lax.rem(strip_at, 2)
    thirds = (
        block(strip_at, strip_at),
        block(jnp.minimum(strip_at + 1, 3), lax.rem(strip_at, 3)),
        block(2 + half_row, half_row),
    )
    for n in (0, 1):
        for t in range(8):
            chunk[8 * n + t] = thirds[n][16 * t : 16 * t + 16]
    lower_half = jnp.where(strip_at < 2, thirds[2][:64], thirds[2][64:])
    for t in range(4):
        chunk[16 + t] = lower_half[16 * t : 16 * t + 16]

    def scatter_copy(turn):
        other, place = peer(turn)
        copy = remote(
            chunk.at[owner(place)],
            pieces.at[shard],
            send_rs.at[other],
            recv_rs.at[shard],
            **place,
        )
        return place, copy

    def scatter_start(turn, _):
        place, copy = scatter_copy(turn)

        @pl.when(owns(place))
        def _():
            copy.start()

        return 0

    over_peers(scatter_start, 0)

    @pl.when(jnp.logical_not(has_columns))
    def _():
        arrived(kept, recv_one.at[2])

    def right_product(k, out):
        for h, width in ((0, 384), (1, 256)):
            total = jnp.zeros((80, width), jnp.float32)
            for at_z in range(4):
                total += bf16_dot(kept[at_z], blocks[h, k, at_z, :, :width], NN)
            out[:, 384 * h : 384 * h + width] = total

    right_product(1 - yl, right_out)
    right_copy = remote(right_out, theirs, send_one.at[3], recv_one.at[3], yl=1 - yl)
    right_copy.start()

    def scatter_arrive(turn, total):
        other, _ = peer(turn)
        arrived(pieces.at[other], recv_rs.at[other])
        return total + pieces[other]

    def spread_copy(turn, flip):
        other, place = peer(turn)
        if flip:
            place = dict(place, yl=1 - place["yl"])
        pair = gram.at[strip_at, owner(own_place)]
        return remote(pair, pair, send_ag.at[flip, other], recv_ag.at[flip, shard], **place)

    def spread_start(turn, _):
        spread_copy(turn, 1).start()
        spread_copy(turn, 0).start()
        return 0

    @pl.when(owns(own_place))
    def _():
        gram[strip_at, owner(own_place)] = over_peers(scatter_arrive, chunk[owner(own_place)])
        over_peers(spread_start, 0)
        spread_copy(22, 1).start()

    right_product(yl, ours)

    def pair_arrives(flip, other, place):
        strip = strip_over if flip else strip_at

        @pl.when(owns(place))
        def _():
            arrived(gram.at[strip, owner(place)], recv_ag.at[flip, other])

    g_copies = []
    for flip, strip in ((1, strip_over), (0, strip_at)):

        def spread_arrive(turn, _):
            other, place = peer(turn)
            pair_arrives(flip, other, place)
            return 0

        if flip:
            pair_arrives(1, shard, own_place)
        over_peers(spread_arrive, 0)
        copy = remote(
            gram.at[strip], gram.at[strip], send_g.at[flip], recv_g.at[strip], core=1 - core
        )
        copy.start()
        g_copies.append(copy)
    for k in (0, 1):
        slot = 2 * k + 1 - core
        arrived(gram.at[slot], recv_g.at[slot])

    arrived(left.at[1 - yl], recv_one.at[1])
    arrived(theirs, recv_one.at[3])

    @pl.when(has_columns)
    def _():
        kept_copy.wait_send()

    def drain(turn, _):
        place, copy = scatter_copy(turn)

        @pl.when(owns(place))
        def _():
            copy.wait_send()

        @pl.when(owns(own_place))
        def _():
            spread_copy(turn, 1).wait_send()
            spread_copy(turn, 0).wait_send()

        return 0

    over_peers(drain, 0)

    @pl.when(owns(own_place))
    def _():
        spread_copy(22, 1).wait_send()

    for copy in sq_copies + core_copies + y_copies + [left_copy, right_copy] + w_copies + g_copies:
        copy.wait_send()
    for copy in waits:
        copy.wait_send()

    @pl.when(yl != yh)
    def _():
        for h in (0, 1):
            for n, (src, dst) in enumerate(pieces_of(h)):
                lend_copy(h, n, src, dst).wait_send()


def gather_and_power(gradient, basis, left_old):
    any_space = pl.BlockSpec(memory_space=pltpu.HBM)
    vmem = pl.BlockSpec(memory_space=pltpu.VMEM)
    dma = pltpu.SemaphoreType.DMA
    f32, bf16 = jnp.float32, jnp.bfloat16
    return pl.pallas_call(
        main_kernel,
        out_shape=(
            jax.ShapeDtypeStruct((4, 20, 16, 128), f32),
            jax.ShapeDtypeStruct((4, 80, 128), f32),
            jax.ShapeDtypeStruct((2, 80, 320), f32),
            jax.ShapeDtypeStruct((4, 8, 128), f32),
            jax.ShapeDtypeStruct((80, 640), f32),
            jax.ShapeDtypeStruct((80, 640), f32),
        ),
        in_specs=[any_space] * 3,
        out_specs=(vmem,) * 6,
        scratch_shapes=[
            pltpu.VMEM((2, 2, 4, 320, 384), bf16),
            pltpu.VMEM((2, 80, 640), bf16),
            pltpu.VMEM((4, 80, 384), f32),
            pltpu.VMEM((8, 128), f32),
            pltpu.VMEM((4, 80, 320), bf16),
            pltpu.VMEM((80, 640), f32),
            pltpu.VMEM((4, 80, 320), f32),
            pltpu.VMEM((4, 80, 320), f32),
            pltpu.VMEM((4, 80, 320), f32),
            pltpu.VMEM((2, 80, 128), f32),
            pltpu.VMEM((2, 80, 128), f32),
            pltpu.VMEM((20, 16, 128), f32),
            pltpu.VMEM((32, 16, 128), f32),
            dma((2, 3)), dma((2, 2, 16)), dma((64,)), dma((4,)), dma((1,)), dma((4,)), dma((2,)),
            dma((4,)), dma((4,)),
            dma((3,)), dma((4,)),
            dma((2,)), dma((4,)),
            dma((5,)), dma((5,)),
            dma((32,)), dma((32,)),
            dma((2, 32)), dma((2, 32)),
            dma((2,)), dma((4,)),
        ],
        compiler_params=pltpu.CompilerParams(
            collective_id=0, has_side_effects=True, vmem_limit_bytes=48 << 20
        ),
    )(*(pltpu.with_memory_space_constraint(v, pltpu.HBM) for v in (gradient, basis, left_old)))


def eliminate(block):
    n = 128
    sub = lax.broadcasted_iota(jnp.int32, (8, n), 0)
    lane = lax.broadcasted_iota(jnp.int32, (8, n), 1)
    m = [block[at : at + 8, :] for at in range(0, n, 8)]

    def columns_of(v, at):
        return [jnp.broadcast_to(v[:, at + j : at + j + 1], (8, n)) for j in range(8)]

    def row_of(v, j):
        return jnp.broadcast_to(v[j : j + 1, :], (8, n))

    cols = columns_of(m[0], 0)
    for b in range(n // 8):
        at = 8 * b
        inside = (lane >= at) & (lane < at + 8)
        rows = m[b]
        ahead = list(range(b + 1, min(b + 4, n // 8)))
        ahead_cols = {i: columns_of(m[i], at) for i in ahead}
        if ahead:
            later = columns_of(rows, at + 8)
            next_later = columns_of(m[b + 1], at + 8)
        ahead_rows = {i: jnp.where(inside, 0.0, m[i]) for i in ahead}
        rows = jnp.where(inside, (lane - at == sub).astype(jnp.float32), rows)
        for j in range(8):
            scale = lax.rsqrt(row_of(cols[j], j))
            below = jnp.where(sub > j, cols[j] * scale, 0.0)
            pivot = row_of(rows, j) * scale
            rows = jnp.where(sub == j, pivot, rows - below * pivot)
            ahead_below = {i: ahead_cols[i][j] * scale for i in ahead}
            for i in ahead:
                ahead_rows[i] = ahead_rows[i] - ahead_below[i] * pivot
            for k in range(j + 1, 8):
                row = row_of(cols[k], j) * scale
                cols[k] = cols[k] - below * row
                for i in ahead:
                    ahead_cols[i][k] = ahead_cols[i][k] - ahead_below[i] * row
            if ahead:
                for k in range(8):
                    row = row_of(later[k], j) * scale
                    later[k] = later[k] - below * row
                    next_later[k] = next_later[k] - ahead_below[b + 1] * row
        m[b] = rows
        for i in ahead:
            m[i] = ahead_rows[i]
        if ahead:
            cols = next_later
        if b + 4 < n // 8:
            change = full_dot(rows, rows, TN)
            for i in range(b + 4, n // 8):
                m[i] = jnp.where(inside, 0.0, m[i]) - change[8 * i : 8 * i + 8, :]
    return jnp.concatenate(m, axis=0)


def factor_kernel(
    gram_ref, w_ref, left_ref, sq_ref, ours_ref, theirs_ref, right_old_ref,
    left_stat_ref, right_stat_ref, q_ref, m_ref,
):
    order = 512
    n = 128
    role = 2 * lax.axis_index("yl") + lax.axis_index("core")
    weight = stat_weight(jnp.sum(sq_ref[0] + sq_ref[1] + sq_ref[2] + sq_ref[3]))[:1, :1]
    left_stat_ref[:, :320] = left_ref[0]
    left_stat_ref[:, 320:] = left_ref[1]
    right_stat_ref[...] = smoothing * right_old_ref[...] + weight * (ours_ref[...] + theirs_ref[...])
    for r in range(4):
        below, half_row = min(r + 1, 3), r % 2
        for t in range(8):
            at = n * r + 16 * t
            m_ref[at : at + 16, n * r : n * r + n] = gram_ref[r, t]
            at = n * below + 16 * t
            m_ref[at : at + 16, n * (r % 3) : n * (r % 3) + n] = gram_ref[r, 8 + t]
        for t in range(4):
            at = n * (2 + half_row) + 64 * (r // 2) + 16 * t
            m_ref[at : at + 16, n * half_row : n * half_row + n] = gram_ref[r, 16 + t]
        m_ref[order:, n * r : n * r + n] = w_ref[r]
    row = lax.broadcasted_iota(jnp.int32, (n, n), 0)
    col = lax.broadcasted_iota(jnp.int32, (n, n), 1)
    for at in range(0, order, n):
        end = at + n
        inverse = jnp.where(col <= row, eliminate(m_ref[at:end, at:end]), 0.0)
        panel = full_dot(m_ref[end:, at:end], inverse, NT)

        @pl.when(role == at // n)
        def _():
            q_ref[...] = panel[order - end :, :]

        for to in range(end, order, n):
            change = full_dot(panel[to - end :, :], panel[to - end : to - end + n, :], NT)
            m_ref[to:, to : to + n] = m_ref[to:, to : to + n] - change


def factor(gram, power, left, squares, ours, theirs, right_old):
    return pl.pallas_call(
        factor_kernel,
        out_shape=(
            jax.ShapeDtypeStruct((80, 640), jnp.float32),
            jax.ShapeDtypeStruct((80, 640), jnp.float32),
            jax.ShapeDtypeStruct((80, 128), jnp.float32),
        ),
        in_specs=[pl.BlockSpec(memory_space=pltpu.VMEM)] * 7,
        out_specs=(pl.BlockSpec(memory_space=pltpu.VMEM),) * 3,
        scratch_shapes=[pltpu.VMEM((592, 512), jnp.float32)],
        compiler_params=pltpu.CompilerParams(vmem_limit_bytes=32 << 20),
    )(gram, power, left, squares, ours, theirs, right_old)


def on_device(gradient, left_old, right_old, basis_old):
    gathered = gather_and_power(gradient, basis_old, left_old)
    return factor(*gathered, right_old)


def solution(mesh):
    finer = Mesh(mesh.devices.reshape(2, 2, 4, 2, 4), ("yl", "core", "z", "yh", "x"))
    return jax.shard_map(
        on_device,
        mesh=finer,
        in_specs=(P(SHARD, ROLE),) * 4,
        out_specs=(P(SHARD, ROLE),) * 3,
        check_vma=False,
    )
```
